256 devices in a mesh: row: 8 (over z_hi, x), col: 32 (over y, z_lo, core).
Axes of the slice: x: 4, y: 4, z: 8 (z_hi: 2, z_lo: 4; z = z_hi * 4 + z_lo), core: 2. Of those that a mesh axis runs over, the one named last changes fastest.
Arguments:
- prior_cov: float32 [16384, 16384], P('row', 'col'), as said below
- diffusivity: float32 [16384], replicated, may hold values from 0.05 to 0.2
- velocity: float32 [2, 16384], replicated, may hold values from -0.3 to 0.3
- process_noise_variance: float32 [16384], replicated, may hold values from 0.2 to 1
- observed_index: int32 [256], replicated, may hold values from 0 to 16383, as said below
- innov_factor: float32 [256, 256], replicated, may hold values from -0.048 to 1.048
Outputs:
- analysis_cov: float32 [16384, 16384], P('row', 'col')
The draws below stay inside these ranges and needn't reach their ends.
Inputs may be any that keep to these rules, and one draw needn't show every extreme that they name: `prior_cov`: symmetric positive definite. `observed_index`: 256 distinct point indices.
All inputs are finite; a program needn't handle non-finite values.
Results may differ from the reference program's by a relative error of at most 0.000098.
Values sent between devices are 32-bit elements; how exact they have to be, the bound alone decides.
A program may use at most 128 MiB of HBM per device.

```python
import math
import jax
import jax.numpy as jnp
from jax import lax

GX = 128
GY = 128
STEPS = 2
NOBS = 256
GRID_POINT_COUNT = 16384


def draw_prior_cov(key, part):
    noise_key, diag_key, amp_key = jax.random.split(jax.random.fold_in(key, 11), 3)
    noise = jax.random.normal(noise_key, (GRID_POINT_COUNT, GRID_POINT_COUNT), jnp.float32)
    diag_vals = jax.random.uniform(diag_key, (GRID_POINT_COUNT,), jnp.float32, 1.0, 2.0)
    amplitude = jax.random.uniform(amp_key, (GRID_POINT_COUNT,), jnp.float32, 0.2, 0.5)
    reach = 6.0
    scale = 0.3 / math.sqrt(GRID_POINT_COUNT)
    labels = jnp.arange(GRID_POINT_COUNT, dtype=jnp.int32)
    grid_row = (labels // GY).astype(jnp.float32)
    grid_col = (labels % GY).astype(jnp.float32)
    root_amp = jnp.sqrt(amplitude)
    across = (grid_row[:, None] - grid_row[None, :]) / reach
    along = (grid_col[:, None] - grid_col[None, :]) / reach
    smooth = root_amp[:, None] * root_amp[None, :] * jnp.exp(-(across * across + along * along))
    symmetric = (noise + noise.T) * scale + smooth
    return symmetric.at[labels, labels].add(diag_vals)


def draw_observed_index(key, part):
    inner_key, order_key = jax.random.split(jax.random.fold_in(key, 23))
    inner = jax.random.permutation(inner_key, GRID_POINT_COUNT - 2)[:NOBS - 2].astype(jnp.int32) + 1
    chosen = jnp.concatenate([jnp.array([0, GRID_POINT_COUNT - 1], jnp.int32), inner])
    return jax.random.permutation(order_key, chosen).astype(jnp.int32)


def draw_innov_factor(key, part):
    diag_key, noise_key = jax.random.split(jax.random.fold_in(key, 37))
    leading = jnp.exp(jax.random.uniform(diag_key, (NOBS,), jnp.float32, math.log(0.5), 0.0))
    noise = jnp.clip(0.012 * jax.random.normal(noise_key, (NOBS, NOBS), jnp.float32), -0.048, 0.048)
    labels = jnp.arange(NOBS, dtype=jnp.int32)
    return noise + jnp.where(labels[:, None] == labels[None, :], leading[:, None], 0.0)


def setup_inputs(seed: int = 0) -> dict:
    keys = jax.random.split(jax.random.key(seed), 7)
    prior_cov = draw_prior_cov(jax.random.fold_in(keys[6], 71), 0)
    diffusivity = jnp.clip(jnp.exp(jax.random.uniform(keys[1], (GRID_POINT_COUNT,), jnp.float32, math.log(0.05), math.log(0.2))), 0.05, 0.2)
    velocity = jnp.clip(jax.random.uniform(keys[2], (2, GRID_POINT_COUNT), jnp.float32, -0.3, 0.3), -0.3, 0.3)
    process_noise_variance = jnp.clip(jnp.exp(jax.random.uniform(keys[3], (GRID_POINT_COUNT,), jnp.float32, math.log(0.2), math.log(1.0))), 0.2, 1.0)
    observed_index = draw_observed_index(jax.random.fold_in(keys[6], 71), 0)
    innov_factor = draw_innov_factor(jax.random.fold_in(keys[6], 71), 0)
    return dict(prior_cov=prior_cov, diffusivity=diffusivity, velocity=velocity, process_noise_variance=process_noise_variance, observed_index=observed_index, innov_factor=innov_factor)


def advect(values, diffuse_coef, east_speed, south_speed, grid_axis):
    extent = values.shape[grid_axis]
    north_side = lax.slice_in_dim(values, 0, extent - 2, axis=grid_axis)
    center = lax.slice_in_dim(values, 1, extent - 1, axis=grid_axis)
    south_side = lax.slice_in_dim(values, 2, extent, axis=grid_axis)
    span_cols = values.shape[grid_axis + 1]
    zero_edge = jnp.zeros_like(lax.slice_in_dim(center, 0, 1, axis=grid_axis + 1))
    east_side = jnp.concatenate([lax.slice_in_dim(center, 1, span_cols, axis=grid_axis + 1), zero_edge], axis=grid_axis + 1)
    west_side = jnp.concatenate([zero_edge, lax.slice_in_dim(center, 0, span_cols - 1, axis=grid_axis + 1)], axis=grid_axis + 1)
    laplace = north_side + south_side + east_side + west_side - 4.0 * center
    return center + diffuse_coef * laplace - 0.5 * east_speed * (east_side - west_side) - 0.5 * south_speed * (south_side - north_side)


def reference(prior_cov, diffusivity, velocity, process_noise_variance, observed_index, innov_factor):
    top_precision = lax.Precision.HIGHEST
    first = prior_cov.reshape(GX, GY, GRID_POINT_COUNT)
    coef_first = (diffusivity.reshape(GX, GY, 1), velocity[0].reshape(GX, GY, 1), velocity[1].reshape(GX, GY, 1))
    for substep in range(STEPS):
        padded = jnp.pad(first, ((1, 1), (0, 0), (0, 0)))
        first = advect(padded, coef_first[0], coef_first[1], coef_first[2], 0)
    second_term = first.reshape(GRID_POINT_COUNT, GX, GY)
    coef_second = (diffusivity.reshape(1, GX, GY), velocity[0].reshape(1, GX, GY), velocity[1].reshape(1, GX, GY))
    for substep in range(STEPS):
        padded = jnp.pad(second_term, ((0, 0), (1, 1), (0, 0)))
        second_term = advect(padded, coef_second[0], coef_second[1], coef_second[2], 1)
    predicted_cov = second_term.reshape(GRID_POINT_COUNT, GRID_POINT_COUNT)
    diagonal_labels = jnp.arange(GRID_POINT_COUNT, dtype=jnp.int32)
    predicted_cov = predicted_cov.at[diagonal_labels, diagonal_labels].add(process_noise_variance)
    column_list = jnp.take(predicted_cov, observed_index, axis=1)
    observed_rows = jnp.take(predicted_cov, observed_index, axis=0)
    left_multiplier = jnp.dot(column_list, innov_factor.T, precision=top_precision, preferred_element_type=jnp.float32)
    right_multiplier = jnp.dot(innov_factor, observed_rows, precision=top_precision, preferred_element_type=jnp.float32)
    return predicted_cov - jnp.dot(left_multiplier, right_multiplier, precision=top_precision, preferred_element_type=jnp.float32)
```

```python
import functools

import jax
import jax.numpy as jnp
from jax import lax
from jax.experimental import pallas as pl
from jax.experimental.pallas import tpu as pltpu
from jax.sharding import PartitionSpec as P

GX = 128
GY = 128
NOBS = 256
ROWS = 2048
COLS = 512
LT = 4
F32 = jnp.float32
BF = jnp.bfloat16
MESH = pl.DeviceIdType.MESH
PAD = 8
VM = pl.BlockSpec(memory_space=pltpu.VMEM)
ANY = pl.BlockSpec(memory_space=pl.ANY)


def split2(v):
    hi = v.astype(BF)
    return hi, (v - hi.astype(F32)).astype(BF)


def dot3(a, b, dims):
    (ah, al), (bh, bl) = split2(a), split2(b)
    dg = functools.partial(
        lax.dot_general, dimension_numbers=(dims, ((), ())), preferred_element_type=F32
    )
    return dg(ah, bh) + (dg(ah, bl) + dg(al, bh))


def coefficients(diffusivity, velocity, variance):
    k, a, b = [t.reshape(GX, GY) for t in (diffusivity, velocity[0], velocity[1])]
    q = variance.reshape(GX, GY)
    lane = lax.broadcasted_iota(jnp.int32, (GX, GY), 1)
    center = 1.0 - 4.0 * k
    north = k + 0.5 * b
    south = k - 0.5 * b
    east = jnp.where(lane < GY - 1, k - 0.5 * a, 0.0)
    west = jnp.where(lane > 0, k + 0.5 * a, 0.0)
    zero = jnp.zeros_like(k)
    rows = jnp.stack([center, north, south, east, west, q, zero, zero], axis=1)
    up = jnp.concatenate([zero[:1], south[:-1]], axis=0)
    down = jnp.concatenate([north[1:], zero[:1]], axis=0)
    before = jnp.concatenate([zero[:, :1], east[:, :-1]], axis=1)
    after = jnp.concatenate([west[:, 1:], zero[:, :1]], axis=1)
    turned = jnp.stack([center, up, down, after, before, zero, zero, zero], axis=1)
    pad = ((PAD, PAD), (0, 0), (0, 0))
    return jnp.pad(rows, pad), jnp.pad(turned, pad)


def spread_rows(coef_ref, first, count, out_ref):
    def body(g, _):
        tile = jnp.transpose(coef_ref[first + g])
        for j in range(5):
            out_ref[j, pl.ds(pl.multiple_of(g * GY, GY), GY), :] = jnp.broadcast_to(
                tile[:, j : j + 1], (GY, GY)
            )
        return 0

    lax.fori_loop(0, count, body, 0)


def row_step(src, coef, base, lt, lead):
    at = pl.multiple_of(base + lead, 8)
    mid = src[lt, pl.ds(at, 8), :]
    north = src[lt, pl.ds(pl.multiple_of(at - GY, 8), 8), :]
    south = src[lt, pl.ds(pl.multiple_of(at + GY, 8), 8), :]
    east = src[lt, pl.ds(at + 1, 8), :]
    west = src[lt, pl.ds(at - 1, 8), :]
    return (coef[0] * mid + coef[1] * north) + (coef[2] * south + (coef[3] * east + coef[4] * west))


def col_two_steps(tiles, coef_ref, first):
    def step(v, g):
        c = [coef_ref[first + g, j : j + 1, :] for j in range(5)]
        east = pltpu.roll(v[g], GY - 1, 1)
        west = pltpu.roll(v[g], 1, 1)
        return (c[0] * v[g] + c[1] * v[g - 1]) + (c[2] * v[g + 1] + (c[3] * east + c[4] * west))

    v1 = {g: step(tiles, g) for g in range(-1, 5)}
    return [step(v1, g) for g in range(4)]


def k0(obs_ref, c_ref, turned_ref, t_ref, e_ref, u_ref, spread_ref):
    r = lax.axis_index("row")
    spread_rows(turned_ref, PAD + 16 * r - 1, 18, spread_ref)
    start = r * ROWS - 2 * GY

    def hot(i, _):
        base = pl.multiple_of(i * 8, 8)
        ids = start + base + lax.broadcasted_iota(jnp.int32, (8, GY), 0)
        for lt in range(2):
            e_ref[lt, pl.ds(base, 8), :] = jnp.where(
                ids == obs_ref[:, lt * GY : (lt + 1) * GY], 1.0, 0.0
            )
        return 0

    lax.fori_loop(0, 2560 // 8, hot, 0)

    def one(i, _):
        base = pl.multiple_of(i * 8, 8)
        coef = [spread_ref[j, pl.ds(base, 8), :] for j in range(5)]
        for lt in range(2):
            u_ref[lt, pl.ds(base, 8), :] = row_step(e_ref, coef, base, lt, GY)
        return 0

    lax.fori_loop(0, 2304 // 8, one, 0)

    def two(i, _):
        base = pl.multiple_of(i * 8, 8)
        coef = [spread_ref[j, pl.ds(pl.multiple_of(base + GY, 8), 8), :] for j in range(5)]
        for lt in range(2):
            e_ref[lt, pl.ds(base, 8), :] = row_step(u_ref, coef, base, lt, GY)
        return 0

    lax.fori_loop(0, ROWS // 8, two, 0)

    def gather(i, _):
        base = pl.multiple_of(i * 512, 512)
        c = c_ref[pl.ds(base, 512), :]
        w = jnp.concatenate([e_ref[lt, pl.ds(base, 512), :] for lt in range(2)], axis=1)
        t = dot3(w, c, ((0,), (0,)))
        for lt in range(LT):
            part = t[:, lt * GY : (lt + 1) * GY]
            t_ref[lt] = jnp.where(i == 0, part, t_ref[lt] + part)
        return 0

    for lt in range(LT):
        t_ref[lt] = jnp.zeros((NOBS, GY), F32)
    lax.fori_loop(0, ROWS // 512, gather, 0)


def ka(
    c_ref,
    t_ref,
    rows_ref,
    obs_ref,
    left_ref,
    right_ref,
    edge_ref,
    halo_ref,
    pc_ref,
    pr_ref,
    ext,
    vb,
    pc,
    pr,
    rs,
    zsum,
    zin,
    text,
    relay1,
    relay2,
    send,
    recv,
    local,
):
    r = lax.axis_index("row")
    c = lax.axis_index("col")
    zh, x = r // 4, r % 4
    y, zl, k = c // 8, (c % 8) // 2, c % 2
    x_edge = jnp.where(zh == 0, 3, 0)
    has_left, has_right = c > 0, c < 31
    partner = (4 * (1 - zh) + x, c)
    x_peers = [(4 * zh + (x + d) % 4, c) for d in (1, 2, 3)]
    y_peers = [(r, 8 * ((y + d) % 4) + 2 * zl + k) for d in (1, 2, 3)]
    z_peers = [(r, 8 * y + 2 * ((zl + d) % 4) + k) for d in (1, 2, 3)]
    core = (r, c + 1 - 2 * k)
    x_to = 2 * (y - 2 * zh) + zl // 2
    gives = (y // 2 == zh) & jnp.logical_not((x_to == x) & (y == x))
    keeps = (y // 2 == zh) & (x_to == x) & (y == x)
    give_to = (4 * zh + jnp.where(gives, x_to, x), 8 * x + 2 * zl + k)
    y_from = 2 * zh + x // 2
    holder = zl // 2 == x % 2
    takes = holder & jnp.logical_not((y_from == y) & (x == y))
    take_from = (4 * zh + y, 8 * y_from + 2 * zl + k)

    def remote(src, dst, s, t, device):
        return pltpu.make_async_remote_copy(
            src_ref=src,
            dst_ref=dst,
            send_sem=send.at[s],
            recv_sem=recv.at[t],
            device_id=device,
            device_id_type=MESH,
        )

    barrier = pltpu.get_barrier_semaphore()

    def greet(device):
        pl.semaphore_signal(barrier, inc=1, device_id=device, device_id_type=MESH)

    for device in x_peers + y_peers + z_peers + [partner, core]:
        greet(device)
    left, right = (r, jnp.maximum(c - 1, 0)), (r, jnp.minimum(c + 1, 31))
    pl.when(has_left)(lambda: greet(left))
    pl.when(has_right)(lambda: greet(right))
    pl.when(gives)(lambda: greet(give_to))
    pl.when(takes)(lambda: greet(take_from))
    one = lambda flag: jnp.where(flag, 1, 0)
    pl.semaphore_wait(
        barrier, 11 + one(has_left) + one(has_right) + one(gives) + one(takes)
    )

    def halo_out(side, piece, t):
        col = GY * t + (256 if side == 1 else 0)
        src = c_ref.at[pl.ds((0, 1792, 256)[piece], 1536 if piece == 2 else 256), pl.ds(col, GY)]
        sem = side * 6 + piece * 2 + t
        device = right if side == 1 else left
        if piece == 2:
            dst = (left_ref if side == 1 else right_ref).at[t]
        else:
            dst = ext.at[t + (0 if side == 1 else 6), pl.ds(256 * piece, 256)]
        return remote(src, dst, sem, sem, device)

    flags = {0: (has_left, has_right), 1: (has_right, has_left)}
    for piece in (0, 1):
        for side in (0, 1):

            @pl.when(flags[side][0])
            def _():
                for t in (0, 1):
                    halo_out(side, piece, t).start()

    inner = [
        pltpu.make_async_copy(
            c_ref.at[pl.ds(1792 * h, 256), pl.ds(GY * t, GY)],
            ext.at[2 + t, pl.ds(256 * h, 256)],
            local.at[4 * h + t],
        )
        for h in (0, 1)
        for t in range(LT)
    ]
    for copy in inner:
        copy.start()

    def rs_copy(d):
        there = (x + d + 1) % 4
        return remote(
            t_ref.at[:, pl.ds(pl.multiple_of(64 * there, 64), 64), :],
            rs.at[d],
            12 + d,
            12 + d,
            x_peers[d],
        )

    for d in range(3):
        rs_copy(d).start()
    for side in (0, 1):

        @pl.when(flags[side][0])
        def _():
            for t in (0, 1):
                halo_out(side, 2, t).start()

    for d in range(3):
        rs_copy(d).wait()
    mine = pl.ds(pl.multiple_of(64 * x, 64), 64)
    for lt in range(LT):
        zsum[lt] = (t_ref[lt, mine, :] + rs[0, lt]) + (rs[1, lt] + rs[2, lt])
    z_copy = remote(zsum, zin, 15, 15, partner)
    z_copy.start()

    for copy in inner:
        copy.wait()
    for side, (there, tiles) in {0: (has_right, (6, 7)), 1: (has_left, (0, 1))}.items():

        @pl.when(there)
        def _():
            for piece in (0, 1):
                for t in (0, 1):
                    halo_out(side, piece, t).wait_recv()

        @pl.when(jnp.logical_not(there))
        def _():
            for t in tiles:
                ext[t] = jnp.zeros((512, GY), F32)

    first = PAD + 4 * c

    def edge(i, _):
        at = pl.ds(pl.multiple_of(i * 16, 16), 16)
        out = col_two_steps({g - 2: ext[g, at, :] for g in range(8)}, rows_ref, first)
        for lt in range(LT):
            vb[lt, at, :] = out[lt]
        return 0

    lax.fori_loop(0, 512 // 16, edge, 0)
    edge_out = pltpu.make_async_copy(vb, edge_ref, local.at[8])
    edge_out.start()

    top, bottom = pl.ds(0, 256), pl.ds(256, 256)
    up_near, down_near = x > 0, x < 3
    up_to = (4 * zh + jnp.maximum(x - 1, 0), c)
    down_to = (4 * zh + jnp.minimum(x + 1, 3), c)
    up_copy = remote(vb.at[:, top], halo_ref.at[:, bottom], 16, 16, up_to)
    down_copy = remote(vb.at[:, bottom], halo_ref.at[:, top], 17, 17, down_to)
    pl.when(up_near)(lambda: up_copy.start())
    pl.when(down_near)(lambda: down_copy.start())
    at_edge = x == x_edge
    far = (4 * zh + x_edge, c)
    cross = pl.ds(pl.multiple_of(jnp.where(zh == 0, 256, 0), 256), 256)
    hop1 = [
        (j, remote(vb.at[j, cross], relay1, 18 + j, 18, (4 * zh + j, c))) for j in range(4)
    ]
    keep1 = pltpu.make_async_copy(vb.at[x, cross], relay1, local.at[9])

    @pl.when(at_edge)
    def _():
        for j, copy in hop1:
            pl.when(x != j)(lambda copy=copy: copy.start())
        keep1.start()

    z_copy.wait()
    for lt in range(LT):
        text[2 + lt] = zsum[lt] + zin[lt]
    t_right = remote(text.at[pl.ds(4, 2)], text.at[pl.ds(0, 2)], 22, 22, right)
    t_left = remote(text.at[pl.ds(2, 2)], text.at[pl.ds(6, 2)], 23, 23, left)
    pl.when(has_right)(lambda: t_right.start())
    pl.when(has_left)(lambda: t_left.start())

    hop2 = remote(relay1, relay2, 24, 24, partner)
    pl.when(at_edge)(lambda: keep1.wait())
    pl.when(jnp.logical_not(at_edge))(lambda: hop1[0][1].wait_recv())
    hop2.start()

    for there, copy, tiles in ((has_left, t_right, (0, 1)), (has_right, t_left, (6, 7))):
        pl.when(there)(lambda copy=copy: copy.wait_recv())

        @pl.when(jnp.logical_not(there))
        def _():
            for t in tiles:
                text[t] = jnp.zeros((64, GY), F32)

    my_obs = obs_ref[mine, :]
    for h in range(4):
        at = pl.ds(16 * h, 16)
        out = col_two_steps({g - 2: text[g, at, :] for g in range(8)}, rows_ref, first)
        for lt in range(LT):
            ids = c * COLS + lt * GY + lax.broadcasted_iota(jnp.int32, (16, GY), 1)
            noise = jnp.broadcast_to(rows_ref[first + lt, 5:6, :], (16, GY))
            zsum[lt, at, :] = out[lt] + jnp.where(my_obs[16 * h : 16 * h + 16] == ids, noise, 0.0)
    p_copy = [remote(zsum, pc.at[:, mine], 25 + d, 25 + d, x_peers[d]) for d in range(3)]
    for copy in p_copy:
        copy.start()
    mine_y = pl.ds(pl.multiple_of(64 * y, 64), 64)
    s = zl % 2
    a_copy = remote(zsum, pr.at[k, s, :, mine], 28, 28, give_to)
    a_keep = pltpu.make_async_copy(zsum, pr.at[k, s, :, mine], local.at[10])
    pl.when(gives)(lambda: a_copy.start())
    pl.when(keeps)(lambda: a_keep.start())
    for lt in range(LT):
        pc[lt, mine, :] = zsum[lt]

    piece = pr.at[k, s, :, mine_y]
    b_copy = [remote(piece, piece, 29 + d, 29 + s, z_peers[d]) for d in range(3)]
    a_wait = remote(zsum, piece, 28, 28, give_to)

    @pl.when(holder)
    def _():
        pl.when(takes)(lambda: a_wait.wait_recv())
        pl.when(jnp.logical_not(takes))(lambda: a_keep.wait())
        for copy in b_copy:
            copy.start()

    for t in range(2):
        other = pr.at[k, t, :, mine_y]
        arrive = remote(other, other, 29, 29 + t, z_peers[0])
        pl.when(jnp.logical_not(holder & (s == t)))(lambda arrive=arrive: arrive.wait_recv())

    hop3 = remote(relay2, halo_ref.at[x, into2(zh)], 38, 38 + 0, far)
    hop2.wait_recv()
    last = pltpu.make_async_copy(relay2, halo_ref.at[x, into2(zh)], local.at[11])
    pl.when(at_edge)(lambda: last.start())

    def forward(j):
        return remote(relay2, halo_ref.at[j, into2(zh)], 38, 38 + j, far)

    for j in range(4):

        @pl.when(jnp.logical_not(at_edge) & (x == j))
        def _():
            forward(j).start()

    slab = pr.at[k, :, :, mine_y]
    c_copy = [remote(slab, slab, 32 + d, 32 + d, y_peers[d]) for d in range(3)]
    for copy in c_copy:
        copy.start()
    for d in range(3):
        there = pl.ds(pl.multiple_of(64 * ((y + 3 - d) % 4), 64), 64)
        slab_in = pr.at[k, :, :, there]
        remote(slab_in, slab_in, 32 + d, 32 + d, y_peers[d]).wait_recv()
    d_copy = remote(pr.at[k], pr.at[k], 35, 35, core)
    d_copy.start()
    for copy in p_copy:
        copy.wait_recv()
    pc_out = pltpu.make_async_copy(pc, pc_ref, local.at[12])
    pc_out.start()
    other = pr.at[1 - k]
    remote(other, other, 35, 35, core).wait_recv()
    pr_out = pltpu.make_async_copy(pr, pr_ref, local.at[13])
    pr_out.start()

    edge_out.wait()
    pl.when(up_near)(lambda: up_copy.wait_send())
    pl.when(down_near)(lambda: down_copy.wait_send())
    pl.when(down_near)(lambda: up_copy.wait_recv())
    pl.when(up_near)(lambda: down_copy.wait_recv())

    @pl.when(at_edge)
    def _():
        for j, copy in hop1:
            pl.when(x != j)(lambda copy=copy: copy.wait_send())
        last.wait()
        for j in range(4):
            pl.when(x != j)(lambda j=j: forward(j).wait_recv())

    hop2.wait_send()
    pl.when(jnp.logical_not(at_edge))(lambda: hop3.wait_send())
    pl.when(has_right)(lambda: t_right.wait_send())
    pl.when(has_left)(lambda: t_left.wait_send())
    for copy in p_copy:
        copy.wait_send()
    pl.when(gives)(lambda: a_copy.wait_send())
    pl.when(keeps & jnp.logical_not(holder))(lambda: a_keep.wait())

    @pl.when(holder)
    def _():
        for copy in b_copy:
            copy.wait_send()

    for copy in c_copy + [d_copy]:
        copy.wait_send()
    for side in (0, 1):
        out_there, in_there = flags[side]

        @pl.when(out_there)
        def _():
            for piece in (0, 1, 2):
                for t in (0, 1):
                    halo_out(side, piece, t).wait_send()

        @pl.when(in_there)
        def _():
            for t in (0, 1):
                halo_out(side, 2, t).wait_recv()

    pc_out.wait()
    pr_out.wait()


def into2(zh):
    return pl.ds(pl.multiple_of(jnp.where(zh == 0, 256, 0), 256), 256)


def kd(
    pc_ref,
    pr_ref,
    f_ref,
    rows_ref,
    c_ref,
    left_ref,
    right_ref,
    edge_ref,
    halo_ref,
    o_ref,
    ext,
    v,
    v1,
    spread_ref,
    out,
    sem,
    osem,
):
    r = lax.axis_index("row")
    c = lax.axis_index("col")
    copies = [
        pltpu.make_async_copy(
            c_ref.at[pl.ds(256, 1536), pl.ds(GY * t, GY)], ext.at[2 + t], sem.at[t]
        )
        for t in range(LT)
    ]
    copies.append(
        pltpu.make_async_copy(edge_ref.at[:, pl.ds(0, 256)], v.at[:, pl.ds(256, 256)], sem.at[4])
    )
    copies.append(
        pltpu.make_async_copy(
            edge_ref.at[:, pl.ds(256, 256)], v.at[:, pl.ds(2048, 256)], sem.at[5]
        )
    )
    for copy in copies:
        copy.start()
    guarded = [
        (c > 0, left_ref, ext.at[pl.ds(0, 2)], sem.at[6]),
        (c < 31, right_ref, ext.at[pl.ds(6, 2)], sem.at[7]),
        (r > 0, halo_ref.at[:, pl.ds(0, 256)], v.at[:, pl.ds(0, 256)], sem.at[8]),
        (r < 7, halo_ref.at[:, pl.ds(256, 256)], v.at[:, pl.ds(2304, 256)], sem.at[9]),
    ]
    for flag, src, dst, s in guarded:

        @pl.when(flag)
        def _():
            pltpu.make_async_copy(src, dst, s).start()

        @pl.when(jnp.logical_not(flag))
        def _():
            dst[...] = jnp.zeros(dst.shape, F32)

    f = f_ref[...]
    g = dot3(f, f, ((0,), (0,)))
    pc = jnp.concatenate([pc_ref[lt] for lt in range(LT)], axis=1)
    w = dot3(g, pc, ((1,), (0,)))
    for ci in range(4):
        lhs = jnp.concatenate([pr_ref[ci % 2, ci // 2, lt] for lt in range(LT)], axis=1)
        u = dot3(lhs, w, ((0,), (0,)))
        for lt in range(LT):
            out[lt, pl.ds(512 * ci, 512), :] = u[:, lt * GY : (lt + 1) * GY]
    spread_rows(rows_ref, PAD + 16 * r - 1, 18, spread_ref)

    for copy in copies:
        copy.wait()
    for flag, src, dst, s in guarded:

        @pl.when(flag)
        def _():
            pltpu.make_async_copy(src, dst, s).wait()

    first = PAD + 4 * c

    def side(i, _):
        at = pl.ds(pl.multiple_of(i * 16, 16), 16)
        res = col_two_steps({g - 2: ext[g, at, :] for g in range(8)}, rows_ref, first)
        for lt in range(LT):
            v[lt, pl.ds(pl.multiple_of(i * 16 + 512, 16), 16), :] = res[lt]
        return 0

    lax.fori_loop(0, 1536 // 16, side, 0)

    def one(i, _):
        base = pl.multiple_of(i * 8, 8)
        coef = [spread_ref[j, pl.ds(base, 8), :] for j in range(5)]
        for lt in range(LT):
            v1[lt, pl.ds(base, 8), :] = row_step(v, coef, base, lt, GY)
        return 0

    lax.fori_loop(0, 2304 // 8, one, 0)

    def store(n):
        return [
            pltpu.make_async_copy(
                out.at[lt, pl.ds(pl.multiple_of(n * 256, 256), 256)],
                o_ref.at[pl.ds(pl.multiple_of(n * 256, 256), 256), pl.ds(GY * lt, GY)],
                osem.at[n, lt],
            )
            for lt in range(LT)
        ]

    def block(n, _):
        def two(i, _):
            base = pl.multiple_of(n * 256 + i * 8, 8)
            coef = [spread_ref[j, pl.ds(pl.multiple_of(base + GY, 8), 8), :] for j in range(5)]
            for lt in range(LT):
                at = pl.ds(base, 8)
                out[lt, at, :] = row_step(v1, coef, base, lt, GY) - out[lt, at, :]
            return 0

        lax.fori_loop(0, 256 // 8, two, 0)

        @pl.when((c // 4 == r) & (n // 2 == c % 4))
        def _():
            i0 = lax.broadcasted_iota(jnp.int32, (GY, GY), 0)
            i1 = lax.broadcasted_iota(jnp.int32, (GY, GY), 1)
            for h in range(2):
                lt = 2 * (n % 2) + h
                at = pl.ds(pl.multiple_of(n * 256 + h * GY, GY), GY)
                noise = jnp.broadcast_to(rows_ref[first + lt, 5:6, :], (GY, GY))
                out[lt, at, :] = out[lt, at, :] + jnp.where(i0 == i1, noise, 0.0)

        for copy in store(n):
            copy.start()
        return 0

    lax.fori_loop(0, ROWS // 256, block, 0)
    for n in range(ROWS // 256):
        for copy in store(n):
            copy.wait()


def on_device(prior_cov, diffusivity, velocity, variance, observed_index, innov_factor):
    rows, turned = coefficients(diffusivity, velocity, variance)
    shape = jax.ShapeDtypeStruct
    limit = 60 * 1024 * 1024
    partial = pl.pallas_call(
        k0,
        out_shape=shape((LT, NOBS, GY), F32),
        in_specs=[VM] * 3,
        out_specs=VM,
        scratch_shapes=[
            pltpu.VMEM((2, 2560, GY), F32),
            pltpu.VMEM((2, 2304, GY), F32),
            pltpu.VMEM((5, 2304, GY), F32),
        ],
        compiler_params=pltpu.CompilerParams(vmem_limit_bytes=limit),
        name="observe",
    )(observed_index.reshape(1, NOBS), prior_cov, turned)
    left, right, edge, halo, pc, pr = pl.pallas_call(
        ka,
        out_shape=[
            shape((2, 1536, GY), F32),
            shape((2, 1536, GY), F32),
            shape((LT, 512, GY), F32),
            shape((LT, 512, GY), F32),
            shape((LT, NOBS, GY), F32),
            shape((2, 2, LT, NOBS, GY), F32),
        ],
        in_specs=[ANY, VM, VM, VM],
        out_specs=[ANY] * 6,
        scratch_shapes=[
            pltpu.VMEM((8, 512, GY), F32),
            pltpu.VMEM((LT, 512, GY), F32),
            pltpu.VMEM((LT, NOBS, GY), F32),
            pltpu.VMEM((2, 2, LT, NOBS, GY), F32),
            pltpu.VMEM((3, LT, 64, GY), F32),
            pltpu.VMEM((LT, 64, GY), F32),
            pltpu.VMEM((LT, 64, GY), F32),
            pltpu.VMEM((8, 64, GY), F32),
            pltpu.VMEM((256, GY), F32),
            pltpu.VMEM((256, GY), F32),
            pltpu.SemaphoreType.DMA((40,)),
            pltpu.SemaphoreType.DMA((42,)),
            pltpu.SemaphoreType.DMA((14,)),
        ],
        compiler_params=pltpu.CompilerParams(
            collective_id=0, has_side_effects=True, vmem_limit_bytes=limit
        ),
        name="exchange",
    )(prior_cov, partial, rows, observed_index.reshape(NOBS, 1))
    return pl.pallas_call(
        kd,
        out_shape=shape((ROWS, COLS), F32),
        in_specs=[VM, VM, VM, VM] + [ANY] * 5,
        out_specs=ANY,
        scratch_shapes=[
            pltpu.VMEM((8, 1536, GY), F32),
            pltpu.VMEM((LT, 2560, GY), F32),
            pltpu.VMEM((LT, 2304, GY), F32),
            pltpu.VMEM((5, 2304, GY), F32),
            pltpu.VMEM((LT, ROWS, GY), F32),
            pltpu.SemaphoreType.DMA((10,)),
            pltpu.SemaphoreType.DMA((ROWS // 256, LT)),
        ],
        compiler_params=pltpu.CompilerParams(vmem_limit_bytes=limit),
        name="update",
    )(pc, pr, innov_factor, rows, prior_cov, left, right, edge, halo)


def solution(mesh):
    return jax.shard_map(
        on_device,
        mesh=mesh,
        in_specs=(P("row", "col"), P(), P(), P(), P(), P()),
        out_specs=P("row", "col"),
        check_vma=False,
    )
```

```python
import functools

import jax
import jax.numpy as jnp
from jax import lax
from jax.experimental import pallas as pl
from jax.experimental.pallas import tpu as pltpu
from jax.sharding import PartitionSpec as P

GX = 128
GY = 128
NOBS = 256
ROWS = 2048
COLS = 512
LT = 4
F32 = jnp.float32
BF = jnp.bfloat16
MESH = pl.DeviceIdType.MESH
PAD = 8
VM = pl.BlockSpec(memory_space=pltpu.VMEM)
ANY = pl.BlockSpec(memory_space=pl.ANY)


def split2(v):
    hi = v.astype(BF)
    return hi, (v - hi.astype(F32)).astype(BF)


def dot3(a, b, dims):
    (ah, al), (bh, bl) = split2(a), split2(b)
    dg = functools.partial(
        lax.dot_general, dimension_numbers=(dims, ((), ())), preferred_element_type=F32
    )
    return dg(ah, bh) + (dg(ah, bl) + dg(al, bh))


def fill_coefficients(k_ref, vel_ref, q_ref, cf):
    k, a, b = k_ref[...], vel_ref[0], vel_ref[1]
    lane = lax.broadcasted_iota(jnp.int32, (GX, GY), 1)
    east = jnp.where(lane < GY - 1, k - 0.5 * a, 0.0)
    west = jnp.where(lane > 0, k + 0.5 * a, 0.0)
    parts = [
        1.0 - 4.0 * k,
        k + 0.5 * b,
        k - 0.5 * b,
        east,
        west,
        q_ref[...],
        pltpu.roll(east, 1, 1),
        pltpu.roll(west, GY - 1, 1),
    ]
    for j, part in enumerate(parts):
        cf[j, 0:PAD] = jnp.zeros((PAD, GY), F32)
        cf[j, PAD : PAD + GX] = part
        cf[j, PAD + GX :] = jnp.zeros((PAD, GY), F32)


def spread_rows(cf, tile, first, count, out_ref):
    def body(g, _):
        for j in range(5):
            tile[j : j + 1, :] = cf[j, pl.ds(first + g, 1), :]
        turned = jnp.transpose(tile[...])
        for j in range(5):
            out_ref[j, pl.ds(pl.multiple_of(g * GY, GY), GY), :] = jnp.broadcast_to(
                turned[:, j : j + 1], (GY, GY)
            )
        return 0

    lax.fori_loop(0, count, body, 0)


def row_step(src, coef, base, lt, lead):
    at = pl.multiple_of(base + lead, 8)
    mid = src[lt, pl.ds(at, 8), :]
    north = src[lt, pl.ds(pl.multiple_of(at - GY, 8), 8), :]
    south = src[lt, pl.ds(pl.multiple_of(at + GY, 8), 8), :]
    east = src[lt, pl.ds(at + 1, 8), :]
    west = src[lt, pl.ds(at - 1, 8), :]
    return (coef[0] * mid + coef[1] * north) + (coef[2] * south + (coef[3] * east + coef[4] * west))


def col_two_steps(tiles, coef_ref, first):
    def step(v, g):
        c = [coef_ref[j, pl.ds(first + g, 1), :] for j in range(5)]
        east = pltpu.roll(v[g], GY - 1, 1)
        west = pltpu.roll(v[g], 1, 1)
        return (c[0] * v[g] + c[1] * v[g - 1]) + (c[2] * v[g + 1] + (c[3] * east + c[4] * west))

    v1 = {g: step(tiles, g) for g in range(-1, 5)}
    return [step(v1, g) for g in range(4)]


def observe(obs_ref, cf, oc, w, ext, t_ref, r):
    for h in range(2):
        ids = jnp.broadcast_to(obs_ref[:, GY * h : GY * (h + 1)].astype(F32), (8, GY))
        oc[GY * h : GY * (h + 1), :] = jnp.broadcast_to(
            jnp.transpose(ids)[:, 0:1], (GY, GY)
        ).astype(jnp.int32)
    lane = lax.broadcasted_iota(jnp.int32, (16, GY), 1)
    first = PAD + 16 * r

    def step(before, v, after, g):
        at = lambda j, n: cf[j, pl.ds(first + n, 1), :]
        east = pltpu.roll(v, GY - 1, 1)
        west = pltpu.roll(v, 1, 1)
        return (at(0, g) * v + at(2, g - 1) * before) + (
            at(1, g + 1) * after + (at(7, g) * east + at(6, g) * west)
        )

    def body(i, _):
        rows = pl.ds(pl.multiple_of(i * 16, 16), 16)
        ids = oc[rows, :] - lane
        e = {g: jnp.where(ids == (16 * r + g) * GY, 1.0, 0.0) for g in range(-2, 18)}
        u = {g: step(e[g - 1], e[g], e[g + 1], g) for g in range(-1, 17)}
        for g in range(16):
            w[rows, GY * g : GY * (g + 1)] = step(u[g - 1], u[g], u[g + 1], g)
        return 0

    lax.fori_loop(0, NOBS // 16, body, 0)
    for n in range(4):
        rows = pl.ds(512 * n, 512)
        block = jnp.concatenate([ext[2 + lt, rows, :] for lt in range(LT)], axis=1)
        t = dot3(w[:, 512 * n : 512 * (n + 1)], block, ((1,), (0,)))
        for lt in range(LT):
            part = t[:, lt * GY : (lt + 1) * GY]
            t_ref[lt] = part if n == 0 else t_ref[lt] + part


PIECES = ((0, 256), (1792, 256), (256, 512), (768, 512), (1280, 512))


def ka(
    c_ref,
    obs_ref,
    k_ref,
    vel_ref,
    q_ref,
    v_ref,
    halo_ref,
    spread_out,
    pc_ref,
    pr_ref,
    ext,
    v,
    spread,
    cf,
    tile,
    oc,
    w,
    t_ref,
    pc,
    pr,
    rs,
    zsum,
    zin,
    text,
    relay1,
    relay2,
    hsend,
    hrecv,
    send,
    recv,
    local,
):
    r = lax.axis_index("row")
    c = lax.axis_index("col")
    zh, x = r // 4, r % 4
    y, zl, k = c // 8, (c % 8) // 2, c % 2
    x_edge = jnp.where(zh == 0, 3, 0)
    has_left, has_right = c > 0, c < 31
    partner = (4 * (1 - zh) + x, c)
    x_peers = [(4 * zh + (x + d) % 4, c) for d in (1, 2, 3)]
    y_peers = [(r, 8 * ((y + d) % 4) + 2 * zl + k) for d in (1, 2, 3)]
    z_peers = [(r, 8 * y + 2 * ((zl + d) % 4) + k) for d in (1, 2, 3)]
    core = (r, c + 1 - 2 * k)
    x_to = 2 * (y - 2 * zh) + zl // 2
    gives = (y // 2 == zh) & jnp.logical_not((x_to == x) & (y == x))
    keeps = (y // 2 == zh) & (x_to == x) & (y == x)
    give_to = (4 * zh + jnp.where(gives, x_to, x), 8 * x + 2 * zl + k)
    y_from = 2 * zh + x // 2
    pair = x % 2
    holder = zl // 2 == pair
    near = zl == 2 - pair
    s = zl % 2
    near_z = (r, 8 * y + 2 * (2 - pair) + k)
    far_z = (r, 8 * y + 6 * (1 - pair) + k)
    twin_z = (r, 8 * y + 2 * (zl + 1 - 2 * s) + k)
    takes = holder & jnp.logical_not((y_from == y) & (x == y))
    take_from = (4 * zh + y, 8 * y_from + 2 * zl + k)

    def remote(src, dst, s, t, device):
        return pltpu.make_async_remote_copy(
            src_ref=src,
            dst_ref=dst,
            send_sem=send.at[s],
            recv_sem=recv.at[t],
            device_id=device,
            device_id_type=MESH,
        )

    barrier = pltpu.get_barrier_semaphore()

    def greet(device):
        pl.semaphore_signal(barrier, inc=1, device_id=device, device_id_type=MESH)

    for device in x_peers + y_peers + z_peers + [partner, core]:
        greet(device)
    left, right = (r, jnp.maximum(c - 1, 0)), (r, jnp.minimum(c + 1, 31))
    pl.when(has_left)(lambda: greet(left))
    pl.when(has_right)(lambda: greet(right))
    pl.when(gives)(lambda: greet(give_to))
    pl.when(takes)(lambda: greet(take_from))
    one = lambda flag: jnp.where(flag, 1, 0)
    pl.semaphore_wait(
        barrier, 11 + one(has_left) + one(has_right) + one(gives) + one(takes)
    )

    def halo_out(side, piece, t):
        start, rows = PIECES[piece]
        src = c_ref.at[pl.ds(start, rows), pl.ds(GY * t + (256 if side == 1 else 0), GY)]
        dst = ext.at[t + (0 if side == 1 else 6), pl.ds(start, rows)]
        sem = side * 10 + piece * 2 + t
        return pltpu.make_async_remote_copy(
            src_ref=src,
            dst_ref=dst,
            send_sem=hsend.at[sem],
            recv_sem=hrecv.at[sem],
            device_id=right if side == 1 else left,
            device_id_type=MESH,
        )

    flags = {0: (has_left, has_right), 1: (has_right, has_left)}

    def halo_start(piece):
        for side in (0, 1):

            @pl.when(flags[side][0])
            def _():
                for t in (0, 1):
                    halo_out(side, piece, t).start()

    def halo_arrive(piece):
        for side in (0, 1):

            @pl.when(flags[side][1])
            def _():
                for t in (0, 1):
                    halo_out(side, piece, t).wait_recv()

    first = PAD + 4 * c

    def transport(piece):
        halo_arrive(piece)
        start, rows = PIECES[piece]

        def body(i, _):
            at = pl.ds(pl.multiple_of(start + i * 16, 16), 16)
            out = col_two_steps({g - 2: ext[g, at, :] for g in range(8)}, cf, first)
            for lt in range(LT):
                v[lt, at, :] = out[lt]
            return 0

        lax.fori_loop(0, rows // 16, body, 0, unroll=2)
        copy = pltpu.make_async_copy(
            v.at[:, pl.ds(start, rows)], v_ref.at[:, pl.ds(start, rows)], local.at[4 + piece]
        )
        copy.start()
        return copy

    halo_start(0)
    halo_start(1)
    inner = [
        pltpu.make_async_copy(c_ref.at[:, pl.ds(GY * t, GY)], ext.at[2 + t], local.at[t])
        for t in range(LT)
    ]
    for copy in inner:
        copy.start()
    halo_start(2)
    for side, tiles in ((0, (6, 7)), (1, (0, 1))):

        @pl.when(jnp.logical_not(flags[side][1]))
        def _():
            for t in tiles:
                ext[t] = jnp.zeros((ROWS, GY), F32)

    fill_coefficients(k_ref, vel_ref, q_ref, cf)
    for copy in inner:
        copy.wait()
    observe(obs_ref, cf, oc, w, ext, t_ref, r)

    def rs_copy(d):
        there = (x + d + 1) % 4
        return remote(
            t_ref.at[:, pl.ds(pl.multiple_of(64 * there, 64), 64), :],
            rs.at[d],
            12 + d,
            12 + d,
            x_peers[d],
        )

    for d in range(3):
        rs_copy(d).start()
    halo_start(3)

    v_out = [transport(0), transport(1)]

    top, bottom = pl.ds(0, 256), pl.ds(1792, 256)
    above, below = pl.ds(0, 256), pl.ds(256, 256)
    up_near, down_near = x > 0, x < 3
    up_to = (4 * zh + jnp.maximum(x - 1, 0), c)
    down_to = (4 * zh + jnp.minimum(x + 1, 3), c)
    up_copy = remote(v.at[:, top], halo_ref.at[:, below], 16, 16, up_to)
    down_copy = remote(v.at[:, bottom], halo_ref.at[:, above], 17, 17, down_to)
    pl.when(up_near)(lambda: up_copy.start())
    pl.when(down_near)(lambda: down_copy.start())
    at_edge = x == x_edge
    far = (4 * zh + x_edge, c)
    cross = pl.ds(pl.multiple_of(jnp.where(zh == 0, 1792, 0), 256), 256)
    hop1 = [
        (j, remote(v.at[j, cross], relay1, 18 + j, 18, (4 * zh + j, c))) for j in range(4)
    ]
    keep1 = pltpu.make_async_copy(v.at[x, cross], relay1, local.at[9])

    @pl.when(at_edge)
    def _():
        for j, copy in hop1:
            pl.when(x != j)(lambda copy=copy: copy.start())
        keep1.start()

    for d in range(3):
        rs_copy(d).wait()
    mine = pl.ds(pl.multiple_of(64 * x, 64), 64)
    for lt in range(LT):
        zsum[lt] = (t_ref[lt, mine, :] + rs[0, lt]) + (rs[1, lt] + rs[2, lt])
    z_copy = remote(zsum, zin, 15, 15, partner)
    z_copy.start()

    spread_rows(cf, tile, PAD + 16 * r - 1, 18, spread)
    spread_copy = pltpu.make_async_copy(spread, spread_out, local.at[14])
    spread_copy.start()

    hop2 = remote(relay1, relay2, 24, 24, partner)
    pl.when(at_edge)(lambda: keep1.wait())
    pl.when(jnp.logical_not(at_edge))(lambda: hop1[0][1].wait_recv())
    hop2.start()

    z_copy.wait()
    for lt in range(LT):
        text[2 + lt] = zsum[lt] + zin[lt]
    t_right = remote(text.at[pl.ds(4, 2)], text.at[pl.ds(0, 2)], 22, 22, right)
    t_left = remote(text.at[pl.ds(2, 2)], text.at[pl.ds(6, 2)], 23, 23, left)
    pl.when(has_right)(lambda: t_right.start())
    pl.when(has_left)(lambda: t_left.start())
    halo_start(4)
    for there, copy, tiles in ((has_left, t_right, (0, 1)), (has_right, t_left, (6, 7))):
        pl.when(there)(lambda copy=copy: copy.wait_recv())

        @pl.when(jnp.logical_not(there))
        def _():
            for t in tiles:
                text[t] = jnp.zeros((64, GY), F32)

    for h in range(4):
        at = pl.ds(16 * h, 16)
        out = col_two_steps({g - 2: text[g, at, :] for g in range(8)}, cf, first)
        for lt in range(LT):
            ids = c * COLS + lt * GY + lax.broadcasted_iota(jnp.int32, (16, GY), 1)
            noise = jnp.broadcast_to(cf[5, pl.ds(first + lt, 1), :], (16, GY))
            my_obs = oc[pl.ds(pl.multiple_of(64 * x + 16 * h, 16), 16), :]
            zsum[lt, at, :] = out[lt] + jnp.where(my_obs == ids, noise, 0.0)
    p_copy = [remote(zsum, pc.at[:, mine], 25 + d, 25 + d, x_peers[d]) for d in range(3)]
    mine_y = pl.ds(pl.multiple_of(64 * y, 64), 64)
    a_copy = remote(zsum, pr.at[k, s, :, mine], 28, 28, give_to)
    a_keep = pltpu.make_async_copy(zsum, pr.at[k, s, :, mine], local.at[10])
    pl.when(gives)(lambda: a_copy.start())
    pl.when(keeps)(lambda: a_keep.start())
    for copy in p_copy:
        copy.start()
    for lt in range(LT):
        pc[lt, mine, :] = zsum[lt]

    piece = pr.at[k, s, :, mine_y]
    slab = pr.at[k, :, :, mine_y]
    b_twin = remote(piece, piece, 29, 29 + s, twin_z)
    b_near = remote(piece, piece, 30, 29 + s, near_z)
    b_far = remote(slab, slab, 31, 31, far_z)
    a_wait = remote(zsum, piece, 28, 28, give_to)

    @pl.when(holder)
    def _():
        pl.when(takes)(lambda: a_wait.wait_recv())
        pl.when(jnp.logical_not(takes))(lambda: a_keep.wait())
        b_near.start()
        b_twin.start()

    v_out.append(transport(2))
    for t in range(2):
        other = pr.at[k, t, :, mine_y]
        arrive = remote(other, other, 29, 29 + t, twin_z)
        pl.when(near | (holder & (s != t)))(lambda arrive=arrive: arrive.wait_recv())
    pl.when(near)(lambda: b_far.start())
    pl.when(jnp.logical_not(near | holder))(lambda: b_far.wait_recv())

    hop3 = remote(relay2, halo_ref.at[x, into2(zh)], 38, 38 + 0, far)
    hop2.wait_recv()
    last = pltpu.make_async_copy(relay2, halo_ref.at[x, into2(zh)], local.at[11])
    pl.when(at_edge)(lambda: last.start())

    def forward(j):
        return remote(relay2, halo_ref.at[j, into2(zh)], 38, 38 + j, far)

    for j in range(4):

        @pl.when(jnp.logical_not(at_edge) & (x == j))
        def _():
            forward(j).start()

    c_copy = [remote(slab, slab, 32 + d, 32 + d, y_peers[d]) for d in range(3)]
    for copy in c_copy:
        copy.start()
    v_out.append(transport(3))
    for d in range(3):
        there = pl.ds(pl.multiple_of(64 * ((y + 3 - d) % 4), 64), 64)
        slab_in = pr.at[k, :, :, there]
        remote(slab_in, slab_in, 32 + d, 32 + d, y_peers[d]).wait_recv()
    d_copy = remote(pr.at[k], pr.at[k], 35, 35, core)
    d_copy.start()
    for copy in p_copy:
        copy.wait_recv()
    pc_out = pltpu.make_async_copy(pc, pc_ref, local.at[12])
    pc_out.start()
    other = pr.at[1 - k]
    remote(other, other, 35, 35, core).wait_recv()
    pr_out = pltpu.make_async_copy(pr, pr_ref, local.at[13])
    pr_out.start()

    v_out.append(transport(4))

    for copy in v_out:
        copy.wait()
    spread_copy.wait()
    pl.when(up_near)(lambda: up_copy.wait_send())
    pl.when(down_near)(lambda: down_copy.wait_send())
    pl.when(down_near)(lambda: up_copy.wait_recv())
    pl.when(up_near)(lambda: down_copy.wait_recv())

    @pl.when(at_edge)
    def _():
        for j, copy in hop1:
            pl.when(x != j)(lambda copy=copy: copy.wait_send())
        last.wait()
        for j in range(4):
            pl.when(x != j)(lambda j=j: forward(j).wait_recv())

    hop2.wait_send()
    pl.when(jnp.logical_not(at_edge))(lambda: hop3.wait_send())
    pl.when(has_right)(lambda: t_right.wait_send())
    pl.when(has_left)(lambda: t_left.wait_send())
    for copy in p_copy:
        copy.wait_send()
    pl.when(gives)(lambda: a_copy.wait_send())

    @pl.when(holder)
    def _():
        b_near.wait_send()
        b_twin.wait_send()

    pl.when(near)(lambda: b_far.wait_send())
    for copy in c_copy + [d_copy]:
        copy.wait_send()
    for side in (0, 1):

        @pl.when(flags[side][0])
        def _():
            for piece in range(5):
                for t in (0, 1):
                    halo_out(side, piece, t).wait_send()

    pc_out.wait()
    pr_out.wait()


def into2(zh):
    return pl.ds(pl.multiple_of(jnp.where(zh == 0, 256, 0), 256), 256)


def kd(pc_ref, pr_ref, f_ref, q_ref, v_in, halo_ref, spread_in, o_ref, v, v1, spread, out, sem, osem):
    r = lax.axis_index("row")
    c = lax.axis_index("col")
    copies = [
        pltpu.make_async_copy(v_in, v.at[:, pl.ds(256, ROWS)], sem.at[0]),
        pltpu.make_async_copy(spread_in, spread, sem.at[1]),
    ]
    for copy in copies:
        copy.start()
    guarded = [
        (r > 0, halo_ref.at[:, pl.ds(0, 256)], v.at[:, pl.ds(0, 256)], sem.at[2]),
        (r < 7, halo_ref.at[:, pl.ds(256, 256)], v.at[:, pl.ds(2304, 256)], sem.at[3]),
    ]
    for flag, src, dst, s in guarded:

        @pl.when(flag)
        def _():
            pltpu.make_async_copy(src, dst, s).start()

        @pl.when(jnp.logical_not(flag))
        def _():
            dst[...] = jnp.zeros(dst.shape, F32)

    f = f_ref[...]
    g = dot3(f, f, ((0,), (0,)))
    pc = jnp.concatenate([pc_ref[lt] for lt in range(LT)], axis=1)
    w = dot3(g, pc, ((1,), (0,)))
    for ci in range(4):
        lhs = jnp.concatenate([pr_ref[ci % 2, ci // 2, lt] for lt in range(LT)], axis=1)
        u = dot3(lhs, w, ((0,), (0,)))
        for lt in range(LT):
            out[lt, pl.ds(512 * ci, 512), :] = u[:, lt * GY : (lt + 1) * GY]

    for copy in copies:
        copy.wait()
    for flag, src, dst, s in guarded:

        @pl.when(flag)
        def _():
            pltpu.make_async_copy(src, dst, s).wait()

    def one(i, _):
        base = pl.multiple_of(i * 8, 8)
        coef = [spread[j, pl.ds(base, 8), :] for j in range(5)]
        for lt in range(LT):
            v1[lt, pl.ds(base, 8), :] = row_step(v, coef, base, lt, GY)
        return 0

    lax.fori_loop(0, 2304 // 8, one, 0, unroll=4)

    def store(n):
        return [
            pltpu.make_async_copy(
                out.at[lt, pl.ds(pl.multiple_of(n * 256, 256), 256)],
                o_ref.at[pl.ds(pl.multiple_of(n * 256, 256), 256), pl.ds(GY * lt, GY)],
                osem.at[n, lt],
            )
            for lt in range(LT)
        ]

    def block(n, _):
        def two(i, _):
            base = pl.multiple_of(n * 256 + i * 8, 8)
            coef = [spread[j, pl.ds(pl.multiple_of(base + GY, 8), 8), :] for j in range(5)]
            for lt in range(LT):
                at = pl.ds(base, 8)
                out[lt, at, :] = row_step(v1, coef, base, lt, GY) - out[lt, at, :]
            return 0

        lax.fori_loop(0, 256 // 8, two, 0, unroll=4)

        @pl.when((c // 4 == r) & (n // 2 == c % 4))
        def _():
            i0 = lax.broadcasted_iota(jnp.int32, (GY, GY), 0)
            i1 = lax.broadcasted_iota(jnp.int32, (GY, GY), 1)
            for h in range(2):
                lt = 2 * (n % 2) + h
                at = pl.ds(pl.multiple_of(n * 256 + h * GY, GY), GY)
                noise = jnp.broadcast_to(q_ref[pl.ds(4 * c + lt, 1), :], (GY, GY))
                out[lt, at, :] = out[lt, at, :] + jnp.where(i0 == i1, noise, 0.0)

        for copy in store(n):
            copy.start()
        return 0

    lax.fori_loop(0, ROWS // 256, block, 0)
    for n in range(ROWS // 256):
        for copy in store(n):
            copy.wait()


def on_device(prior_cov, diffusivity, velocity, variance, observed_index, innov_factor):
    shape = jax.ShapeDtypeStruct
    limit = 60 * 1024 * 1024
    k = diffusivity.reshape(GX, GY)
    vel = velocity.reshape(2, GX, GY)
    q = variance.reshape(GX, GY)
    v, halo, spread, pc, pr = pl.pallas_call(
        ka,
        out_shape=[
            shape((LT, ROWS, GY), F32),
            shape((LT, 512, GY), F32),
            shape((5, 2304, GY), F32),
            shape((LT, NOBS, GY), F32),
            shape((2, 2, LT, NOBS, GY), F32),
        ],
        in_specs=[ANY, VM, VM, VM, VM],
        out_specs=[ANY] * 5,
        scratch_shapes=[
            pltpu.VMEM((8, ROWS, GY), F32),
            pltpu.VMEM((LT, ROWS, GY), F32),
            pltpu.VMEM((5, 2304, GY), F32),
            pltpu.VMEM((8, GX + 2 * PAD, GY), F32),
            pltpu.VMEM((8, GY), F32),
            pltpu.VMEM((NOBS, GY), jnp.int32),
            pltpu.VMEM((NOBS, ROWS), F32),
            pltpu.VMEM((LT, NOBS, GY), F32),
            pltpu.VMEM((LT, NOBS, GY), F32),
            pltpu.VMEM((2, 2, LT, NOBS, GY), F32),
            pltpu.VMEM((3, LT, 64, GY), F32),
            pltpu.VMEM((LT, 64, GY), F32),
            pltpu.VMEM((LT, 64, GY), F32),
            pltpu.VMEM((8, 64, GY), F32),
            pltpu.VMEM((256, GY), F32),
            pltpu.VMEM((256, GY), F32),
            pltpu.SemaphoreType.DMA((20,)),
            pltpu.SemaphoreType.DMA((20,)),
            pltpu.SemaphoreType.DMA((40,)),
            pltpu.SemaphoreType.DMA((42,)),
            pltpu.SemaphoreType.DMA((15,)),
        ],
        compiler_params=pltpu.CompilerParams(
            collective_id=0, has_side_effects=True, vmem_limit_bytes=limit
        ),
        name="exchange",
    )(prior_cov, observed_index.reshape(1, NOBS), k, vel, q)
    return pl.pallas_call(
        kd,
        out_shape=shape((ROWS, COLS), F32),
        in_specs=[VM] * 4 + [ANY] * 3,
        out_specs=ANY,
        scratch_shapes=[
            pltpu.VMEM((LT, 2560, GY), F32),
            pltpu.VMEM((LT, 2304, GY), F32),
            pltpu.VMEM((5, 2304, GY), F32),
            pltpu.VMEM((LT, ROWS, GY), F32),
            pltpu.SemaphoreType.DMA((4,)),
            pltpu.SemaphoreType.DMA((ROWS // 256, LT)),
        ],
        compiler_params=pltpu.CompilerParams(vmem_limit_bytes=limit),
        name="update",
    )(pc, pr, innov_factor, q, v, halo, spread)


def solution(mesh):
    return jax.shard_map(
        on_device,
        mesh=mesh,
        in_specs=(P("row", "col"), P(), P(), P(), P(), P()),
        out_specs=P("row", "col"),
        check_vma=False,
    )
```

```python
import functools

import jax
import jax.numpy as jnp
from jax import lax
from jax.experimental import pallas as pl
from jax.experimental.pallas import tpu as pltpu
from jax.sharding import PartitionSpec as P

GX = 128
GY = 128
NOBS = 256
ROWS = 2048
COLS = 512
LT = 4
F32 = jnp.float32
BF = jnp.bfloat16
MESH = pl.DeviceIdType.MESH
PAD = 8
VM = pl.BlockSpec(memory_space=pltpu.VMEM)
ANY = pl.BlockSpec(memory_space=pl.ANY)


def split2(v):
    hi = v.astype(BF)
    return hi, (v - hi.astype(F32)).astype(BF)


def dot3(a, b, dims):
    (ah, al), (bh, bl) = split2(a), split2(b)
    dg = functools.partial(
        lax.dot_general, dimension_numbers=(dims, ((), ())), preferred_element_type=F32
    )
    return dg(ah, bh) + (dg(ah, bl) + dg(al, bh))


def fill_coefficients(k_ref, vel_ref, q_ref, speed, cf):
    for j in range(2):
        for g in range(GX):
            speed[j, g : g + 1, :] = vel_ref[j : j + 1, GY * g : GY * (g + 1)]
    k, a, b = k_ref[...], speed[0], speed[1]
    lane = lax.broadcasted_iota(jnp.int32, (GX, GY), 1)
    east = jnp.where(lane < GY - 1, k - 0.5 * a, 0.0)
    west = jnp.where(lane > 0, k + 0.5 * a, 0.0)
    parts = [
        1.0 - 4.0 * k,
        k + 0.5 * b,
        k - 0.5 * b,
        east,
        west,
        q_ref[...],
        pltpu.roll(east, 1, 1),
        pltpu.roll(west, GY - 1, 1),
    ]
    for j, part in enumerate(parts):
        cf[j, 0:PAD] = jnp.zeros((PAD, GY), F32)
        cf[j, PAD : PAD + GX] = part
        cf[j, PAD + GX :] = jnp.zeros((PAD, GY), F32)


def spread_rows(cf, tile, first, count, out_ref):
    def body(g, _):
        for j in range(5):
            tile[j : j + 1, :] = cf[j, pl.ds(first + g, 1), :]
        turned = jnp.transpose(tile[...])
        for j in range(5):
            out_ref[j, pl.ds(pl.multiple_of(g * GY, GY), GY), :] = jnp.broadcast_to(
                turned[:, j : j + 1], (GY, GY)
            )
        return 0

    lax.fori_loop(0, count, body, 0)


def row_step(src, coef, base, lt, lead):
    at = pl.multiple_of(base + lead, 8)
    mid = src[lt, pl.ds(at, 8), :]
    north = src[lt, pl.ds(pl.multiple_of(at - GY, 8), 8), :]
    south = src[lt, pl.ds(pl.multiple_of(at + GY, 8), 8), :]
    east = src[lt, pl.ds(at + 1, 8), :]
    west = src[lt, pl.ds(at - 1, 8), :]
    return (coef[0] * mid + coef[1] * north) + (coef[2] * south + (coef[3] * east + coef[4] * west))


def col_two_steps(tiles, coef_ref, first):
    def step(v, g):
        c = [coef_ref[j, pl.ds(first + g, 1), :] for j in range(5)]
        east = pltpu.roll(v[g], GY - 1, 1)
        west = pltpu.roll(v[g], 1, 1)
        return (c[0] * v[g] + c[1] * v[g - 1]) + (c[2] * v[g + 1] + (c[3] * east + c[4] * west))

    v1 = {g: step(tiles, g) for g in range(-1, 5)}
    return [step(v1, g) for g in range(4)]


def observe(obs_ref, cf, oc, w, ext, t_ref, r):
    for h in range(2):
        ids = jnp.broadcast_to(obs_ref[:, GY * h : GY * (h + 1)].astype(F32), (8, GY))
        oc[GY * h : GY * (h + 1), :] = jnp.broadcast_to(
            jnp.transpose(ids)[:, 0:1], (GY, GY)
        ).astype(jnp.int32)
    lane = lax.broadcasted_iota(jnp.int32, (32, GY), 1)
    first = PAD + 16 * r

    def step(before, v, after, g):
        at = lambda j, n: cf[j, pl.ds(first + n, 1), :]
        east = pltpu.roll(v, GY - 1, 1)
        west = pltpu.roll(v, 1, 1)
        return (at(0, g) * v + at(2, g - 1) * before) + (
            at(1, g + 1) * after + (at(7, g) * east + at(6, g) * west)
        )

    def body(i, _):
        rows = pl.ds(pl.multiple_of(i * 32, 32), 32)
        ids = oc[rows, :] - lane
        e = {g: jnp.where(ids == (16 * r + g) * GY, 1.0, 0.0) for g in range(-2, 18)}
        u = {g: step(e[g - 1], e[g], e[g + 1], g) for g in range(-1, 17)}
        for g in range(16):
            w[rows, GY * g : GY * (g + 1)] = step(u[g - 1], u[g], u[g + 1], g)
        return 0

    lax.fori_loop(0, NOBS // 32, body, 0)
    for n in range(4):
        rows = pl.ds(512 * n, 512)
        block = jnp.concatenate([ext[2 + lt, rows, :] for lt in range(LT)], axis=1)
        t = dot3(w[:, 512 * n : 512 * (n + 1)], block, ((1,), (0,)))
        for lt in range(LT):
            part = t[:, lt * GY : (lt + 1) * GY]
            t_ref[lt] = part if n == 0 else t_ref[lt] + part


PIECES = (0, 1792, 256, 512, 768, 1024, 1280, 1536)


def ka(
    c_ref,
    obs_ref,
    k_ref,
    vel_ref,
    q_ref,
    f_ref,
    p_ref,
    ext,
    v,
    v1,
    out,
    spread,
    cf,
    speed,
    tile,
    oc,
    w,
    t_ref,
    pc,
    pr,
    rs,
    psum,
    zin,
    text,
    relay1,
    relay2,
    hsend,
    hrecv,
    send,
    recv,
    local,
):
    r = lax.axis_index("row")
    c = lax.axis_index("col")
    zh, x = r // 4, r % 4
    y, zl, k = c // 8, (c % 8) // 2, c % 2
    no = jnp.logical_not
    x_edge = jnp.where(zh == 0, 3, 0)
    has_left, has_right = c > 0, c < 31
    c_left, c_right = jnp.maximum(c - 1, 0), jnp.minimum(c + 1, 31)
    r_far = 4 * (1 - zh) + x
    left, right, partner = (r, c_left), (r, c_right), (r_far, c)
    left_far, right_far = (r_far, c_left), (r_far, c_right)
    x_peers = [(4 * zh + (x + d) % 4, c) for d in (1, 2, 3)]
    y_peers = [(r, 8 * ((y + d) % 4) + 2 * zl + k) for d in (1, 2, 3)]
    z_peers = [(r, 8 * y + 2 * ((zl + d) % 4) + k) for d in (1, 2, 3)]
    core = (r, c + 1 - 2 * k)
    x_to = 2 * (y - 2 * zh) + zl // 2
    keeps = (y // 2 == zh) & (x_to == x) & (y == x)
    gives = (y // 2 == zh) & no(keeps)
    give_to = (4 * zh + jnp.where(gives, x_to, x), 8 * x + 2 * zl + k)
    y_from = 2 * zh + x // 2
    pair = x % 2
    holder = zl // 2 == pair
    near = zl == 2 - pair
    far = no(holder | near)
    takes = holder & no((y_from == y) & (x == y))
    take_from = (4 * zh + y, 8 * y_from + 2 * zl + k)
    s = zl % 2
    near_z = (r, 8 * y + 2 * (2 - pair) + k)
    far_z = (r, 8 * y + 6 * (1 - pair) + k)
    twin_z = (r, 8 * y + 2 * (zl + 1 - 2 * s) + k)

    def remote(src, dst, i, j, device, h=0):
        return pltpu.make_async_remote_copy(
            src_ref=src,
            dst_ref=dst,
            send_sem=send.at[h, i],
            recv_sem=recv.at[h, j],
            device_id=device,
            device_id_type=MESH,
        )

    halves = range(2)

    def rows_of(h, n):
        return pl.ds(pl.multiple_of(128 * h + 32 * n, 32), 32)

    barrier = pltpu.get_barrier_semaphore()

    def greet(*devices):
        for device in devices:
            pl.semaphore_signal(barrier, inc=1, device_id=device, device_id_type=MESH)

    greet(*x_peers, *y_peers, *z_peers, partner, core)
    pl.when(has_left)(lambda: greet(left, left_far))
    pl.when(has_right)(lambda: greet(right, right_far))
    pl.when(gives)(lambda: greet(give_to))
    pl.when(takes)(lambda: greet(take_from))
    one = lambda flag: jnp.where(flag, 1, 0)
    pl.semaphore_wait(
        barrier, 11 + 2 * one(has_left) + 2 * one(has_right) + one(gives) + one(takes)
    )

    def halo_out(side, piece, t):
        rows = pl.ds(PIECES[piece], 256)
        sem = side * 16 + piece * 2 + t
        return pltpu.make_async_remote_copy(
            src_ref=c_ref.at[rows, pl.ds(GY * t + (256 if side == 1 else 0), GY)],
            dst_ref=ext.at[t + (0 if side == 1 else 6), rows],
            send_sem=hsend.at[sem],
            recv_sem=hrecv.at[sem],
            device_id=right if side == 1 else left,
            device_id_type=MESH,
        )

    flags = {0: (has_left, has_right), 1: (has_right, has_left)}

    def halo_start(piece):
        for side in (0, 1):

            @pl.when(flags[side][0])
            def _():
                for t in (0, 1):
                    halo_out(side, piece, t).start()

    first = PAD + 4 * c

    def transport(piece):
        for side in (0, 1):

            @pl.when(flags[side][1])
            def _():
                for t in (0, 1):
                    halo_out(side, piece, t).wait_recv()

        def body(i, _):
            at = pl.ds(pl.multiple_of(PIECES[piece] + i * 16, 16), 16)
            to = pl.ds(pl.multiple_of(PIECES[piece] + 256 + i * 16, 16), 16)
            res = col_two_steps({g - 2: ext[g, at, :] for g in range(8)}, cf, first)
            for lt in range(LT):
                v[lt, to, :] = res[lt]
            return 0

        lax.fori_loop(0, 256 // 16, body, 0, unroll=2)

    def along_rows(one, two):
        def step_one(i, _):
            base = pl.multiple_of(i * 8, 8)
            coef = [spread[j, pl.ds(base, 8), :] for j in range(5)]
            for lt in range(LT):
                v1[lt, pl.ds(base, 8), :] = row_step(v, coef, base, lt, GY)
            return 0

        def step_two(i, _):
            base = pl.multiple_of(i * 8, 8)
            at = pl.ds(base, 8)
            coef = [spread[j, pl.ds(pl.multiple_of(base + GY, 8), 8), :] for j in range(5)]
            for lt in range(LT):
                out[lt, at, :] = out[lt, at, :] + row_step(v1, coef, base, lt, GY)
            return 0

        if one:
            lax.fori_loop((one[0] + 1) * 16, (one[1] + 1) * 16, step_one, 0, unroll=4)
        if two:
            lax.fori_loop(two[0] * 16, two[1] * 16, step_two, 0, unroll=4)

    def begin_out():
        def clear(i, _):
            for lt in range(LT):
                out[lt, pl.ds(pl.multiple_of(i * 64, 64), 64), :] = jnp.zeros((64, GY), F32)
            return 0

        lax.fori_loop(0, ROWS // 64, clear, 0)

        @pl.when(c // 4 == r)
        def _():
            i0 = lax.broadcasted_iota(jnp.int32, (GY, GY), 0)
            i1 = lax.broadcasted_iota(jnp.int32, (GY, GY), 1)
            for lt in range(LT):
                at = pl.ds(pl.multiple_of(512 * (c % 4) + GY * lt, GY), GY)
                noise = jnp.broadcast_to(cf[5, pl.ds(first + lt, 1), :], (GY, GY))
                out[lt, at, :] = jnp.where(i0 == i1, noise, 0.0)

    def subtract(kk, s_, weights):
        ci = 2 * s_ + kk
        lhs = jnp.concatenate([pr[kk, s_, lt] for lt in range(LT)], axis=1)
        u = dot3(lhs, weights, ((0,), (0,)))
        at = pl.ds(pl.multiple_of(512 * ci, 512), 512)
        for lt in range(LT):
            out[lt, at, :] = out[lt, at, :] - u[:, lt * GY : (lt + 1) * GY]

    halo_start(0)
    halo_start(1)
    inner = [
        pltpu.make_async_copy(c_ref.at[:, pl.ds(GY * t, GY)], ext.at[2 + t], local.at[t])
        for t in range(LT)
    ]
    for copy in inner:
        copy.start()
    halo_start(2)
    fill_coefficients(k_ref, vel_ref, q_ref, speed, cf)
    for copy in inner:
        copy.wait()
    observe(obs_ref, cf, oc, w, ext, t_ref, r)

    def rs_copy(h, d):
        there = rows_of(h, (x + d + 1) % 4)
        return remote(t_ref.at[:, there, :], rs.at[h, d], 12 + d, 12 + d, x_peers[d], h)

    for h in halves:
        for d in range(3):
            rs_copy(h, d).start()
    halo_start(3)
    for side, tiles in ((0, (6, 7)), (1, (0, 1))):

        @pl.when(no(flags[side][1]))
        def _():
            for t in tiles:
                ext[t] = jnp.zeros((ROWS, GY), F32)
                for h in halves:
                    text[h, t] = jnp.zeros((32, GY), F32)
                    zin[h, t] = jnp.zeros((32, GY), F32)

    transport(0)
    transport(1)
    top, bottom = pl.ds(256, 256), pl.ds(2048, 256)
    above, below = pl.ds(0, 256), pl.ds(2304, 256)
    up_near, down_near = x > 0, x < 3
    up_to = (4 * zh + jnp.maximum(x - 1, 0), c)
    down_to = (4 * zh + jnp.minimum(x + 1, 3), c)
    up_copy = remote(v.at[:, top], v.at[:, below], 16, 16, up_to)
    down_copy = remote(v.at[:, bottom], v.at[:, above], 17, 17, down_to)
    pl.when(up_near)(lambda: up_copy.start())
    pl.when(down_near)(lambda: down_copy.start())
    at_edge = x == x_edge
    edge = (4 * zh + x_edge, c)
    cross = pl.ds(pl.multiple_of(jnp.where(zh == 0, 2048, 256), 256), 256)
    into = pl.ds(pl.multiple_of(jnp.where(zh == 0, 2304, 0), 256), 256)
    hop1 = [remote(v.at[j, cross], relay1, 18 + j, 18, (4 * zh + j, c)) for j in range(4)]
    keep1 = pltpu.make_async_copy(v.at[x, cross], relay1, local.at[4])

    @pl.when(at_edge)
    def _():
        for j, copy in enumerate(hop1):
            pl.when(x != j)(lambda copy=copy: copy.start())
        keep1.start()

    whole, low, high = pl.ds(2, 4), pl.ds(2, 2), pl.ds(4, 2)
    before, after = pl.ds(0, 2), pl.ds(6, 2)
    z_copy, to_right, to_left = [], [], []
    for h in halves:
        for d in range(3):
            rs_copy(h, d).wait()
        for lt in range(LT):
            text[h, 2 + lt] = (t_ref[lt, rows_of(h, x), :] + rs[h, 0, lt]) + (
                rs[h, 1, lt] + rs[h, 2, lt]
            )
        z_copy.append(remote(text.at[h, whole], zin.at[h, whole], 15, 15, partner, h))
        to_right += [
            remote(text.at[h, high], zin.at[h, before], 48, 48, right_far, h),
            remote(text.at[h, high], text.at[h, before], 22, 22, right, h),
        ]
        to_left += [
            remote(text.at[h, low], zin.at[h, after], 49, 49, left_far, h),
            remote(text.at[h, low], text.at[h, after], 23, 23, left, h),
        ]
        z_copy[h].start()

        @pl.when(has_right)
        def _():
            for copy in to_right[-2:]:
                copy.start()

        @pl.when(has_left)
        def _():
            for copy in to_left[-2:]:
                copy.start()

    halo_start(4)
    spread_rows(cf, tile, PAD + 16 * r - 1, 18, spread)
    begin_out()

    a_copy, a_keep, p_copy = [], [], []
    for h in halves:
        z_copy[h].wait_recv()

        @pl.when(has_left)
        def _():
            for copy in to_right[2 * h : 2 * h + 2]:
                copy.wait_recv()

        @pl.when(has_right)
        def _():
            for copy in to_left[2 * h : 2 * h + 2]:
                copy.wait_recv()

        for i in range(2):
            at = pl.ds(16 * i, 16)
            total = {g - 2: text[h, g, at, :] + zin[h, g, at, :] for g in range(8)}
            res = col_two_steps(total, cf, first)
            my_obs = oc[pl.ds(pl.multiple_of(128 * h + 32 * x + 16 * i, 16), 16), :]
            for lt in range(LT):
                ids = c * COLS + lt * GY + lax.broadcasted_iota(jnp.int32, (16, GY), 1)
                noise = jnp.broadcast_to(cf[5, pl.ds(first + lt, 1), :], (16, GY))
                psum[h, lt, at, :] = res[lt] + jnp.where(my_obs == ids, noise, 0.0)
        a_copy.append(remote(psum.at[h], pr.at[k, s, :, rows_of(h, x)], 28, 28, give_to, h))
        a_keep.append(
            pltpu.make_async_copy(psum.at[h], pr.at[k, s, :, rows_of(h, x)], local.at[13 + h])
        )
        pl.when(gives)(lambda: a_copy[h].start())
        pl.when(keeps)(lambda: a_keep[h].start())
    for h in halves:
        for d in range(3):
            p_copy.append(
                remote(psum.at[h], pc.at[:, rows_of(h, x)], 25 + d, 25 + d, x_peers[d], h)
            )
            p_copy[-1].start()
        for lt in range(LT):
            pc[lt, rows_of(h, x), :] = psum[h, lt]
    halo_start(5)

    hop2 = remote(relay1, relay2, 24, 24, partner)
    pl.when(at_edge)(lambda: keep1.wait())
    pl.when(no(at_edge))(lambda: hop1[0].wait_recv())
    hop2.start()
    transport(2)
    halo_start(6)

    t0 = jnp.where(holder, s, 1 - pair)
    kinds = (t0, 1 - t0)

    def part(h, i, d, kk):
        return pr.at[kk, kinds[i], :, rows_of(h, (y + 4 - d) % 4)]

    piece = [pr.at[k, s, :, rows_of(h, y)] for h in halves]
    a_wait = [remote(psum.at[h], piece[h], 28, 28, give_to, h) for h in halves]
    b_twin = [remote(piece[h], piece[h], 29, 30, twin_z, h) for h in halves]
    second = jnp.where(s == 1 - pair, 0, 1)
    b_near = [remote(piece[h], piece[h], 30, 29 + second, near_z, h) for h in halves]
    arrive = [
        [remote(part(h, i, 0, k), part(h, i, 0, k), 31 + i, 29 + i, far_z, h) for i in range(2)]
        for h in halves
    ]

    def along_y(h, i, d):
        n = 33 + 2 * d + i
        return remote(part(h, i, 0, k), part(h, i, 0, k), n, n, y_peers[d], h)

    def y_in(h, i, d):
        n = 33 + 2 * d + i
        return remote(part(h, i, d + 1, k), part(h, i, d + 1, k), n, n, y_peers[d], h)

    def to_core(h, i, d):
        n = 40 + 2 * d + i
        return remote(part(h, i, d, k), part(h, i, d, k), n, n, core, h)

    def core_in(h, i, d):
        n = 40 + 2 * d + i
        return remote(part(h, i, d, 1 - k), part(h, i, d, 1 - k), n, n, core, h)

    def pass_on(h, i):
        pl.when(near)(lambda: arrive[h][i].start())
        for d in range(3):
            along_y(h, i, d).start()
        to_core(h, i, 0).start()

    for h in halves:

        @pl.when(holder)
        def _():
            pl.when(takes)(lambda: a_wait[h].wait_recv())
            pl.when(no(takes))(lambda: a_keep[h].wait())
            b_near[h].start()
            b_twin[h].start()

        @pl.when(no(holder))
        def _():
            arrive[h][0].wait_recv()

        pass_on(h, 0)
    halo_start(7)
    for h in halves:
        arrive[h][1].wait_recv()
        pass_on(h, 1)

    transport(3)
    along_rows((1, 5), (2, 4))
    hop2.wait_recv()
    last = pltpu.make_async_copy(relay2, v.at[x, into], local.at[6])
    pl.when(at_edge)(lambda: last.start())

    def forward(j):
        return remote(relay2, v.at[j, into], 39, 52 + j, edge)

    for j in range(4):
        pl.when(no(at_edge) & (x == j))(lambda j=j: forward(j).start())

    for i in range(2):
        for h in halves:
            for d in range(3):
                y_in(h, i, d).wait_recv()
                to_core(h, i, d + 1).start()
        transport(4 + i)
        along_rows((5 + 2 * i, 7 + 2 * i), (4 + 2 * i, 6 + 2 * i))
    for copy in p_copy:
        copy.wait_recv()
    f = f_ref[...]
    gain = dot3(f, f, ((0,), (0,)))
    weights = dot3(gain, jnp.concatenate([pc[lt] for lt in range(LT)], axis=1), ((1,), (0,)))
    for i in range(2):
        subtract(k, i, weights)
    transport(6)
    along_rows((9, 11), (8, 10))
    for h in halves:
        for i in range(2):
            for d in range(4):
                core_in(h, i, d).wait_recv()
    for i in range(2):
        subtract(1 - k, i, weights)

    def store(n):
        rows = pl.ds(*((256, 1024), (1280, 768), (0, 256))[n])
        return pltpu.make_async_copy(out.at[:, rows], p_ref.at[:, rows], local.at[7 + n])

    store(0).start()
    transport(7)
    along_rows((11, 15), (10, 14))
    pl.when(down_near)(lambda: up_copy.wait_recv())
    pl.when(up_near)(lambda: down_copy.wait_recv())

    @pl.when(at_edge)
    def _():
        last.wait()
        for j in range(4):
            pl.when(x != j)(lambda j=j: forward(j).wait_recv())

    for flag, rows in ((r == 0, above), (r == 7, below)):

        @pl.when(flag)
        def _():
            for lt in range(LT):
                v[lt, rows, :] = jnp.zeros((256, GY), F32)

    along_rows((15, 17), (14, 16))
    store(1).start()
    along_rows((-1, 1), (0, 2))
    store(2).start()

    for n in range(3):
        store(n).wait()
    pl.when(up_near)(lambda: up_copy.wait_send())
    pl.when(down_near)(lambda: down_copy.wait_send())

    @pl.when(at_edge)
    def _():
        for j, copy in enumerate(hop1):
            pl.when(x != j)(lambda copy=copy: copy.wait_send())

    hop2.wait_send()
    pl.when(no(at_edge))(lambda: forward(0).wait_send())
    for copy in z_copy:
        copy.wait_send()

    @pl.when(has_right)
    def _():
        for copy in to_right:
            copy.wait_send()

    @pl.when(has_left)
    def _():
        for copy in to_left:
            copy.wait_send()

    for copy in p_copy:
        copy.wait_send()
    for h in halves:
        pl.when(gives)(lambda: a_copy[h].wait_send())
        pl.when(keeps & no(holder))(lambda: a_keep[h].wait())

        @pl.when(holder)
        def _():
            b_near[h].wait_send()
            b_twin[h].wait_send()

        for i in range(2):
            pl.when(near)(lambda: arrive[h][i].wait_send())
            for d in range(3):
                along_y(h, i, d).wait_send()
            for d in range(4):
                to_core(h, i, d).wait_send()
    for side in (0, 1):

        @pl.when(flags[side][0])
        def _():
            for n in range(len(PIECES)):
                for t in (0, 1):
                    halo_out(side, n, t).wait_send()


def kd(p_in, o_ref, p, sem, osem):
    chunks = [(lt, pl.ds(1024 * n, 1024)) for n in range(2) for lt in range(LT)]
    loads = [
        pltpu.make_async_copy(p_in.at[lt, at], p.at[lt, at], sem.at[n])
        for n, (lt, at) in enumerate(chunks)
    ]
    stores = [
        pltpu.make_async_copy(p.at[lt, at], o_ref.at[at, pl.ds(GY * lt, GY)], osem.at[n])
        for n, (lt, at) in enumerate(chunks)
    ]
    for copy in loads:
        copy.start()
    for load, put in zip(loads, stores):
        load.wait()
        put.start()
    for copy in stores:
        copy.wait()


def on_device(prior_cov, diffusivity, velocity, variance, observed_index, innov_factor):
    shape = jax.ShapeDtypeStruct
    limit = 60 * 1024 * 1024
    k = diffusivity.reshape(GX, GY)
    q = variance.reshape(GX, GY)
    p = pl.pallas_call(
        ka,
        out_shape=shape((LT, ROWS, GY), F32),
        in_specs=[ANY] + [VM] * 5,
        out_specs=ANY,
        scratch_shapes=[
            pltpu.VMEM((8, ROWS, GY), F32),
            pltpu.VMEM((LT, 2560, GY), F32),
            pltpu.VMEM((LT, 2304, GY), F32),
            pltpu.VMEM((LT, ROWS, GY), F32),
            pltpu.VMEM((5, 2304, GY), F32),
            pltpu.VMEM((8, GX + 2 * PAD, GY), F32),
            pltpu.VMEM((2, GX, GY), F32),
            pltpu.VMEM((8, GY), F32),
            pltpu.VMEM((NOBS, GY), jnp.int32),
            pltpu.VMEM((NOBS, ROWS), F32),
            pltpu.VMEM((LT, NOBS, GY), F32),
            pltpu.VMEM((LT, NOBS, GY), F32),
            pltpu.VMEM((2, 2, LT, NOBS, GY), F32),
            pltpu.VMEM((2, 3, LT, 32, GY), F32),
            pltpu.VMEM((2, LT, 32, GY), F32),
            pltpu.VMEM((2, 8, 32, GY), F32),
            pltpu.VMEM((2, 8, 32, GY), F32),
            pltpu.VMEM((256, GY), F32),
            pltpu.VMEM((256, GY), F32),
            pltpu.SemaphoreType.DMA((32,)),
            pltpu.SemaphoreType.DMA((32,)),
            pltpu.SemaphoreType.DMA((2, 56)),
            pltpu.SemaphoreType.DMA((2, 56)),
            pltpu.SemaphoreType.DMA((15,)),
        ],
        compiler_params=pltpu.CompilerParams(
            collective_id=0, has_side_effects=True, vmem_limit_bytes=limit
        ),
        name="exchange",
    )(prior_cov, observed_index.reshape(1, NOBS), k, velocity, q, innov_factor)
    return pl.pallas_call(
        kd,
        out_shape=shape((ROWS, COLS), F32),
        in_specs=[ANY],
        out_specs=ANY,
        scratch_shapes=[
            pltpu.VMEM((LT, ROWS, GY), F32),
            pltpu.SemaphoreType.DMA((8,)),
            pltpu.SemaphoreType.DMA((8,)),
        ],
        compiler_params=pltpu.CompilerParams(vmem_limit_bytes=limit),
        name="place",
    )(p)


def solution(mesh):
    return jax.shard_map(
        on_device,
        mesh=mesh,
        in_specs=(P("row", "col"), P(), P(), P(), P(), P()),
        out_specs=P("row", "col"),
        check_vma=False,
    )
```

```python
import functools

import jax
import jax.numpy as jnp
from jax import lax
from jax.experimental import pallas as pl
from jax.experimental.pallas import tpu as pltpu
from jax.sharding import PartitionSpec as P

GX = 128
GY = 128
NOBS = 256
ROWS = 2048
COLS = 512
LT = 4
F32 = jnp.float32
BF = jnp.bfloat16
MESH = pl.DeviceIdType.MESH
PAD = 8
VM = pl.BlockSpec(memory_space=pltpu.VMEM)
HBM = pl.BlockSpec(memory_space=pltpu.HBM)
ANY = pl.BlockSpec(memory_space=pl.ANY)


def split2(v):
    hi = v.astype(BF)
    return hi, (v - hi.astype(F32)).astype(BF)


def dot3(a, b, dims):
    (ah, al), (bh, bl) = split2(a), split2(b)
    dg = functools.partial(
        lax.dot_general, dimension_numbers=(dims, ((), ())), preferred_element_type=F32
    )
    return dg(ah, bh) + (dg(ah, bl) + dg(al, bh))


def fill_coefficients(k_ref, vel_ref, q_ref, speed, cf):
    for j in range(2):
        for g in range(GX):
            speed[j, g : g + 1, :] = vel_ref[j : j + 1, GY * g : GY * (g + 1)]
    k, a, b = k_ref[...], speed[0], speed[1]
    lane = lax.broadcasted_iota(jnp.int32, (GX, GY), 1)
    east = jnp.where(lane < GY - 1, k - 0.5 * a, 0.0)
    west = jnp.where(lane > 0, k + 0.5 * a, 0.0)
    parts = [
        1.0 - 4.0 * k,
        k + 0.5 * b,
        k - 0.5 * b,
        east,
        west,
        q_ref[...],
        pltpu.roll(east, 1, 1),
        pltpu.roll(west, GY - 1, 1),
    ]
    for j, part in enumerate(parts):
        cf[j, 0:PAD] = jnp.zeros((PAD, GY), F32)
        cf[j, PAD : PAD + GX] = part
        cf[j, PAD + GX :] = jnp.zeros((PAD, GY), F32)


def spread_rows(cf, tile, first, count, out_ref):
    def body(g, _):
        for j in range(5):
            tile[j : j + 1, :] = cf[j, pl.ds(first + g, 1), :]
        turned = jnp.transpose(tile[...])
        for j in range(5):
            out_ref[j, pl.ds(pl.multiple_of(g * GY, GY), GY), :] = jnp.broadcast_to(
                turned[:, j : j + 1], (GY, GY)
            )
        return 0

    lax.fori_loop(0, count, body, 0)


def row_step(src, coef, base, lt, lead):
    at = pl.multiple_of(base + lead, 8)
    mid = src[lt, pl.ds(at, 8), :]
    north = src[lt, pl.ds(pl.multiple_of(at - GY, 8), 8), :]
    south = src[lt, pl.ds(pl.multiple_of(at + GY, 8), 8), :]
    east = src[lt, pl.ds(at + 1, 8), :]
    west = src[lt, pl.ds(at - 1, 8), :]
    return (coef[0] * mid + coef[1] * north) + (coef[2] * south + (coef[3] * east + coef[4] * west))


def col_two_steps(tiles, coef_ref, first):
    def step(v, g):
        c = [coef_ref[j, pl.ds(first + g, 1), :] for j in range(5)]
        east = pltpu.roll(v[g], GY - 1, 1)
        west = pltpu.roll(v[g], 1, 1)
        return (c[0] * v[g] + c[1] * v[g - 1]) + (c[2] * v[g + 1] + (c[3] * east + c[4] * west))

    v1 = {g: step(tiles, g) for g in range(-1, 5)}
    return [step(v1, g) for g in range(4)]


def observe(obs_ref, cf, oc, w, ext, t_ref, r):
    for h in range(2):
        ids = jnp.broadcast_to(obs_ref[:, GY * h : GY * (h + 1)].astype(F32), (8, GY))
        oc[GY * h : GY * (h + 1), :] = jnp.broadcast_to(
            jnp.transpose(ids)[:, 0:1], (GY, GY)
        ).astype(jnp.int32)
    lane = lax.broadcasted_iota(jnp.int32, (32, GY), 1)
    first = PAD + 16 * r

    def step(before, v, after, g):
        at = lambda j, n: cf[j, pl.ds(first + n, 1), :]
        east = pltpu.roll(v, GY - 1, 1)
        west = pltpu.roll(v, 1, 1)
        return (at(0, g) * v + at(2, g - 1) * before) + (
            at(1, g + 1) * after + (at(7, g) * east + at(6, g) * west)
        )

    def body(i, _):
        rows = pl.ds(pl.multiple_of(i * 32, 32), 32)
        ids = oc[rows, :] - lane
        e = {g: jnp.where(ids == (16 * r + g) * GY, 1.0, 0.0) for g in range(-2, 18)}
        u = {g: step(e[g - 1], e[g], e[g + 1], g) for g in range(-1, 17)}
        for g in range(16):
            w[rows, GY * g : GY * (g + 1)] = step(u[g - 1], u[g], u[g + 1], g)
        return 0

    lax.fori_loop(0, NOBS // 32, body, 0)
    for n in range(4):
        rows = pl.ds(512 * n, 512)
        block = jnp.concatenate([ext[2 + lt, rows, :] for lt in range(LT)], axis=1)
        t = dot3(w[:, 512 * n : 512 * (n + 1)], block, ((1,), (0,)))
        for lt in range(LT):
            part = t[:, lt * GY : (lt + 1) * GY]
            t_ref[lt] = part if n == 0 else t_ref[lt] + part


PIECES = (0, 1792, 256, 512, 768, 1024, 1280, 1536)


def ka(
    c_ref,
    obs_ref,
    k_ref,
    vel_ref,
    q_ref,
    f_ref,
    out,
    ext,
    v,
    v1,
    spread,
    cf,
    speed,
    tile,
    oc,
    w,
    t_ref,
    pc,
    pr,
    rs,
    psum,
    zin,
    text,
    relay1,
    relay2,
    hsend,
    hrecv,
    send,
    recv,
    local,
):
    r = lax.axis_index("row")
    c = lax.axis_index("col")
    zh, x = r // 4, r % 4
    y, zl, k = c // 8, (c % 8) // 2, c % 2
    no = jnp.logical_not
    x_edge = jnp.where(zh == 0, 3, 0)
    has_left, has_right = c > 0, c < 31
    c_left, c_right = jnp.maximum(c - 1, 0), jnp.minimum(c + 1, 31)
    left, right, partner = (r, c_left), (r, c_right), (4 * (1 - zh) + x, c)
    x_peers = [(4 * zh + (x + d) % 4, c) for d in (1, 2, 3)]
    y_peers = [(r, 8 * ((y + d) % 4) + 2 * zl + k) for d in (1, 2, 3)]
    z_peers = [(r, 8 * y + 2 * ((zl + d) % 4) + k) for d in (1, 2, 3)]
    core = (r, c + 1 - 2 * k)
    x_to = 2 * (y - 2 * zh) + zl // 2
    keeps = (y // 2 == zh) & (x_to == x) & (y == x)
    gives = (y // 2 == zh) & no(keeps)
    give_to = (4 * zh + jnp.where(gives, x_to, x), 8 * x + 2 * zl + k)
    y_from = 2 * zh + x // 2
    pair = x % 2
    holder = zl // 2 == pair
    near = zl == 2 - pair
    far = no(holder | near)
    takes = holder & no((y_from == y) & (x == y))
    take_from = (4 * zh + y, 8 * y_from + 2 * zl + k)
    s = zl % 2
    near_z = (r, 8 * y + 2 * (2 - pair) + k)
    far_z = (r, 8 * y + 6 * (1 - pair) + k)
    twin_z = (r, 8 * y + 2 * (zl + 1 - 2 * s) + k)

    def remote(src, dst, i, j, device, h=0):
        return pltpu.make_async_remote_copy(
            src_ref=src,
            dst_ref=dst,
            send_sem=send.at[h, i],
            recv_sem=recv.at[h, j],
            device_id=device,
            device_id_type=MESH,
        )

    halves = range(2)

    def rows_of(h, n):
        return pl.ds(pl.multiple_of(128 * h + 32 * n, 32), 32)

    barrier = pltpu.get_barrier_semaphore()

    def greet(*devices):
        for device in devices:
            pl.semaphore_signal(barrier, inc=1, device_id=device, device_id_type=MESH)

    greet(*x_peers, *y_peers, *z_peers, partner, core)
    pl.when(has_left)(lambda: greet(left))
    pl.when(has_right)(lambda: greet(right))
    pl.when(gives)(lambda: greet(give_to))
    pl.when(takes)(lambda: greet(take_from))
    one = lambda flag: jnp.where(flag, 1, 0)
    pl.semaphore_wait(
        barrier, 11 + one(has_left) + one(has_right) + one(gives) + one(takes)
    )

    def halo_out(side, piece, t):
        rows = pl.ds(PIECES[piece], 256)
        sem = side * 16 + piece * 2 + t
        return pltpu.make_async_remote_copy(
            src_ref=c_ref.at[rows, pl.ds(GY * t + (256 if side == 1 else 0), GY)],
            dst_ref=ext.at[t + (0 if side == 1 else 6), rows],
            send_sem=hsend.at[sem],
            recv_sem=hrecv.at[sem],
            device_id=right if side == 1 else left,
            device_id_type=MESH,
        )

    flags = {0: (has_left, has_right), 1: (has_right, has_left)}

    def halo_start(piece):
        for side in (0, 1):

            @pl.when(flags[side][0])
            def _():
                for t in (0, 1):
                    halo_out(side, piece, t).start()

    first = PAD + 4 * c

    def transport(piece):
        for side in (0, 1):

            @pl.when(flags[side][1])
            def _():
                for t in (0, 1):
                    halo_out(side, piece, t).wait_recv()

        def body(i, _):
            at = pl.ds(pl.multiple_of(PIECES[piece] + i * 16, 16), 16)
            to = pl.ds(pl.multiple_of(PIECES[piece] + 256 + i * 16, 16), 16)
            res = col_two_steps({g - 2: ext[g, at, :] for g in range(8)}, cf, first)
            for lt in range(LT):
                v[lt, to, :] = res[lt]
            return 0

        lax.fori_loop(0, 256 // 16, body, 0, unroll=2)

    def along_rows(one, two):
        def step_one(i, _):
            base = pl.multiple_of(i * 8, 8)
            coef = [spread[j, pl.ds(base, 8), :] for j in range(5)]
            for lt in range(LT):
                v1[lt, pl.ds(base, 8), :] = row_step(v, coef, base, lt, GY)
            return 0

        def step_two(i, _):
            base = pl.multiple_of(i * 8, 8)
            at = pl.ds(base, 8)
            coef = [spread[j, pl.ds(pl.multiple_of(base + GY, 8), 8), :] for j in range(5)]
            for lt in range(LT):
                out[lt, at, :] = out[lt, at, :] + row_step(v1, coef, base, lt, GY)
            return 0

        if one:
            lax.fori_loop((one[0] + 1) * 16, (one[1] + 1) * 16, step_one, 0, unroll=4)
        if two:
            lax.fori_loop(two[0] * 16, two[1] * 16, step_two, 0, unroll=4)

    def begin_out():
        def clear(i, _):
            for lt in range(LT):
                out[lt, pl.ds(pl.multiple_of(i * 64, 64), 64), :] = jnp.zeros((64, GY), F32)
            return 0

        lax.fori_loop(0, ROWS // 64, clear, 0)

        @pl.when(c // 4 == r)
        def _():
            i0 = lax.broadcasted_iota(jnp.int32, (GY, GY), 0)
            i1 = lax.broadcasted_iota(jnp.int32, (GY, GY), 1)
            for lt in range(LT):
                at = pl.ds(pl.multiple_of(512 * (c % 4) + GY * lt, GY), GY)
                noise = jnp.broadcast_to(cf[5, pl.ds(first + lt, 1), :], (GY, GY))
                out[lt, at, :] = jnp.where(i0 == i1, noise, 0.0)

    def subtract(kk, s_, weights):
        ci = 2 * s_ + kk
        lhs = jnp.concatenate([pr[kk, s_, lt] for lt in range(LT)], axis=1)
        u = dot3(lhs, weights, ((0,), (0,)))
        at = pl.ds(pl.multiple_of(512 * ci, 512), 512)
        for lt in range(LT):
            out[lt, at, :] = out[lt, at, :] - u[:, lt * GY : (lt + 1) * GY]

    halo_start(0)
    halo_start(1)
    inner = [
        pltpu.make_async_copy(c_ref.at[:, pl.ds(GY * t, GY)], ext.at[2 + t], local.at[t])
        for t in range(LT)
    ]
    for copy in inner:
        copy.start()
    halo_start(2)
    fill_coefficients(k_ref, vel_ref, q_ref, speed, cf)
    for copy in inner:
        copy.wait()
    observe(obs_ref, cf, oc, w, ext, t_ref, r)

    def rs_copy(h, d):
        there = rows_of(h, (x + d + 1) % 4)
        return remote(t_ref.at[:, there, :], rs.at[h, d], 12 + d, 12 + d, x_peers[d], h)

    for h in halves:
        for d in range(3):
            rs_copy(h, d).start()
    halo_start(3)
    for side, tiles in ((0, (6, 7)), (1, (0, 1))):

        @pl.when(no(flags[side][1]))
        def _():
            for t in tiles:
                ext[t] = jnp.zeros((ROWS, GY), F32)
                for h in halves:
                    text[h, t] = jnp.zeros((32, GY), F32)

    transport(0)
    transport(1)
    top, bottom = pl.ds(256, 256), pl.ds(2048, 256)
    above, below = pl.ds(0, 256), pl.ds(2304, 256)
    up_near, down_near = x > 0, x < 3
    up_to = (4 * zh + jnp.maximum(x - 1, 0), c)
    down_to = (4 * zh + jnp.minimum(x + 1, 3), c)
    up_copy = remote(v.at[:, top], v.at[:, below], 16, 16, up_to)
    down_copy = remote(v.at[:, bottom], v.at[:, above], 17, 17, down_to)
    pl.when(up_near)(lambda: up_copy.start())
    pl.when(down_near)(lambda: down_copy.start())
    at_edge = x == x_edge
    edge = (4 * zh + x_edge, c)
    cross = pl.ds(pl.multiple_of(jnp.where(zh == 0, 2048, 256), 256), 256)
    into = pl.ds(pl.multiple_of(jnp.where(zh == 0, 2304, 0), 256), 256)
    hop1 = [remote(v.at[j, cross], relay1, 18 + j, 18, (4 * zh + j, c)) for j in range(4)]
    keep1 = pltpu.make_async_copy(v.at[x, cross], relay1, local.at[4])

    @pl.when(at_edge)
    def _():
        for j, copy in enumerate(hop1):
            pl.when(x != j)(lambda copy=copy: copy.start())
        keep1.start()

    whole, low, high = pl.ds(2, 4), pl.ds(2, 2), pl.ds(4, 2)
    before, after = pl.ds(0, 2), pl.ds(6, 2)
    z_copy, to_right, to_left = [], [], []
    for h in halves:
        for d in range(3):
            rs_copy(h, d).wait()
        for lt in range(LT):
            text[h, 2 + lt] = (t_ref[lt, rows_of(h, x), :] + rs[h, 0, lt]) + (
                rs[h, 1, lt] + rs[h, 2, lt]
            )
        z_copy.append(remote(text.at[h, whole], zin.at[h], 15, 15, partner, h))
        to_right.append(remote(text.at[h, high], text.at[h, before], 22, 22, right, h))
        to_left.append(remote(text.at[h, low], text.at[h, after], 23, 23, left, h))
        z_copy[h].start()

    halo_start(4)
    spread_rows(cf, tile, PAD + 16 * r - 1, 18, spread)
    for h in halves:
        z_copy[h].wait()
        for lt in range(LT):
            text[h, 2 + lt] = text[h, 2 + lt] + zin[h, lt]
        pl.when(has_right)(lambda: to_right[h].start())
        pl.when(has_left)(lambda: to_left[h].start())
    begin_out()

    a_copy, a_keep, p_copy = [], [], []
    for h in halves:
        pl.when(has_left)(lambda: to_right[h].wait_recv())
        pl.when(has_right)(lambda: to_left[h].wait_recv())
        for i in range(2):
            at = pl.ds(16 * i, 16)
            total = {g - 2: text[h, g, at, :] for g in range(8)}
            res = col_two_steps(total, cf, first)
            my_obs = oc[pl.ds(pl.multiple_of(128 * h + 32 * x + 16 * i, 16), 16), :]
            for lt in range(LT):
                ids = c * COLS + lt * GY + lax.broadcasted_iota(jnp.int32, (16, GY), 1)
                noise = jnp.broadcast_to(cf[5, pl.ds(first + lt, 1), :], (16, GY))
                psum[h, lt, at, :] = res[lt] + jnp.where(my_obs == ids, noise, 0.0)
        a_copy.append(remote(psum.at[h], pr.at[k, s, :, rows_of(h, x)], 28, 28, give_to, h))
        a_keep.append(
            pltpu.make_async_copy(psum.at[h], pr.at[k, s, :, rows_of(h, x)], local.at[13 + h])
        )
        pl.when(gives)(lambda: a_copy[h].start())
        pl.when(keeps)(lambda: a_keep[h].start())
    for h in halves:
        for d in range(3):
            p_copy.append(
                remote(psum.at[h], pc.at[:, rows_of(h, x)], 25 + d, 25 + d, x_peers[d], h)
            )
            p_copy[-1].start()
        for lt in range(LT):
            pc[lt, rows_of(h, x), :] = psum[h, lt]

    hop2 = remote(relay1, relay2, 24, 24, partner)
    pl.when(at_edge)(lambda: keep1.wait())
    pl.when(no(at_edge))(lambda: hop1[0].wait_recv())
    hop2.start()
    transport(2)

    t0 = jnp.where(holder, s, 1 - pair)
    kinds = (t0, 1 - t0)

    def part(h, i, d, kk):
        return pr.at[kk, kinds[i], :, rows_of(h, (y + 4 - d) % 4)]

    piece = [pr.at[k, s, :, rows_of(h, y)] for h in halves]
    a_wait = [remote(psum.at[h], piece[h], 28, 28, give_to, h) for h in halves]
    b_twin = [remote(piece[h], piece[h], 29, 30, twin_z, h) for h in halves]
    second = jnp.where(s == 1 - pair, 0, 1)
    b_near = [remote(piece[h], piece[h], 30, 29 + second, near_z, h) for h in halves]
    arrive = [
        [remote(part(h, i, 0, k), part(h, i, 0, k), 31 + i, 29 + i, far_z, h) for i in range(2)]
        for h in halves
    ]

    def along_y(h, i, d):
        n = 33 + 2 * d + i
        return remote(part(h, i, 0, k), part(h, i, 0, k), n, n, y_peers[d], h)

    def y_in(h, i, d):
        n = 33 + 2 * d + i
        return remote(part(h, i, d + 1, k), part(h, i, d + 1, k), n, n, y_peers[d], h)

    def to_core(h, i, d):
        n = 40 + 2 * d + i
        return remote(part(h, i, d, k), part(h, i, d, k), n, n, core, h)

    def core_in(h, i, d):
        n = 40 + 2 * d + i
        return remote(part(h, i, d, 1 - k), part(h, i, d, 1 - k), n, n, core, h)

    def pass_on(h, i):
        pl.when(near)(lambda: arrive[h][i].start())
        for d in range(3):
            along_y(h, i, d).start()
        to_core(h, i, 0).start()

    for h in halves:

        @pl.when(holder)
        def _():
            pl.when(takes)(lambda: a_wait[h].wait_recv())
            pl.when(no(takes))(lambda: a_keep[h].wait())
            b_near[h].start()
            b_twin[h].start()

        @pl.when(no(holder))
        def _():
            arrive[h][0].wait_recv()

        pass_on(h, 0)
    halo_start(5)
    for h in halves:
        arrive[h][1].wait_recv()
        pass_on(h, 1)

    halo_start(6)
    halo_start(7)

    transport(3)
    along_rows((1, 5), (2, 4))
    hop2.wait_recv()
    last = pltpu.make_async_copy(relay2, v.at[x, into], local.at[6])
    pl.when(at_edge)(lambda: last.start())

    def forward(j):
        return remote(relay2, v.at[j, into], 39, 52 + j, edge)

    for j in range(4):
        pl.when(no(at_edge) & (x == j))(lambda j=j: forward(j).start())

    for i in range(2):
        for h in halves:
            for d in range(3):
                y_in(h, i, d).wait_recv()
                to_core(h, i, d + 1).start()
        transport(4 + i)
        along_rows((5 + 2 * i, 7 + 2 * i), (4 + 2 * i, 6 + 2 * i))
    for copy in p_copy:
        copy.wait_recv()
    f = f_ref[...]
    gain = dot3(f, f, ((0,), (0,)))
    weights = dot3(gain, jnp.concatenate([pc[lt] for lt in range(LT)], axis=1), ((1,), (0,)))
    for i in range(2):
        subtract(k, i, weights)
    transport(6)
    along_rows((9, 11), (8, 10))
    for h in halves:
        for i in range(2):
            for d in range(4):
                core_in(h, i, d).wait_recv()
    for i in range(2):
        subtract(1 - k, i, weights)

    pl.when(down_near)(lambda: up_copy.wait_recv())
    pl.when(up_near)(lambda: down_copy.wait_recv())

    @pl.when(at_edge)
    def _():
        last.wait()
        for j in range(4):
            pl.when(x != j)(lambda j=j: forward(j).wait_recv())

    for flag, rows in ((r == 0, above), (r == 7, below)):

        @pl.when(flag)
        def _():
            for lt in range(LT):
                v[lt, rows, :] = jnp.zeros((256, GY), F32)

    along_rows((-1, 1), (0, 2))
    transport(7)
    along_rows((11, 15), (10, 14))
    along_rows((15, 17), (14, 16))

    pl.when(up_near)(lambda: up_copy.wait_send())
    pl.when(down_near)(lambda: down_copy.wait_send())

    @pl.when(at_edge)
    def _():
        for j, copy in enumerate(hop1):
            pl.when(x != j)(lambda copy=copy: copy.wait_send())

    hop2.wait_send()
    pl.when(no(at_edge))(lambda: forward(0).wait_send())

    @pl.when(has_right)
    def _():
        for copy in to_right:
            copy.wait_send()

    @pl.when(has_left)
    def _():
        for copy in to_left:
            copy.wait_send()

    for copy in p_copy:
        copy.wait_send()
    for h in halves:
        pl.when(gives)(lambda: a_copy[h].wait_send())
        pl.when(keeps & no(holder))(lambda: a_keep[h].wait())

        @pl.when(holder)
        def _():
            b_near[h].wait_send()
            b_twin[h].wait_send()

        for i in range(2):
            pl.when(near)(lambda: arrive[h][i].wait_send())
            for d in range(3):
                along_y(h, i, d).wait_send()
            for d in range(4):
                to_core(h, i, d).wait_send()
    for side in (0, 1):

        @pl.when(flags[side][0])
        def _():
            for n in range(len(PIECES)):
                for t in (0, 1):
                    halo_out(side, n, t).wait_send()


def kd(p_ref, o_ref, sem):
    stores = [
        pltpu.make_async_copy(p_ref.at[lt], o_ref.at[:, pl.ds(GY * lt, GY)], sem.at[lt])
        for lt in range(LT)
    ]
    for copy in stores:
        copy.start()
    for copy in stores:
        copy.wait()


def on_device(prior_cov, diffusivity, velocity, variance, observed_index, innov_factor):
    shape = jax.ShapeDtypeStruct
    limit = 48 * 1024 * 1024
    k = diffusivity.reshape(GX, GY)
    q = variance.reshape(GX, GY)
    p = pl.pallas_call(
        ka,
        out_shape=shape((LT, ROWS, GY), F32),
        in_specs=[HBM] + [VM] * 5,
        out_specs=VM,
        scratch_shapes=[
            pltpu.VMEM((8, ROWS, GY), F32),
            pltpu.VMEM((LT, 2560, GY), F32),
            pltpu.VMEM((LT, 2304, GY), F32),
            pltpu.VMEM((5, 2304, GY), F32),
            pltpu.VMEM((8, GX + 2 * PAD, GY), F32),
            pltpu.VMEM((2, GX, GY), F32),
            pltpu.VMEM((8, GY), F32),
            pltpu.VMEM((NOBS, GY), jnp.int32),
            pltpu.VMEM((NOBS, ROWS), F32),
            pltpu.VMEM((LT, NOBS, GY), F32),
            pltpu.VMEM((LT, NOBS, GY), F32),
            pltpu.VMEM((2, 2, LT, NOBS, GY), F32),
            pltpu.VMEM((2, 3, LT, 32, GY), F32),
            pltpu.VMEM((2, LT, 32, GY), F32),
            pltpu.VMEM((2, LT, 32, GY), F32),
            pltpu.VMEM((2, 8, 32, GY), F32),
            pltpu.VMEM((256, GY), F32),
            pltpu.VMEM((256, GY), F32),
            pltpu.SemaphoreType.DMA((32,)),
            pltpu.SemaphoreType.DMA((32,)),
            pltpu.SemaphoreType.DMA((2, 56)),
            pltpu.SemaphoreType.DMA((2, 56)),
            pltpu.SemaphoreType.DMA((15,)),
        ],
        compiler_params=pltpu.CompilerParams(
            collective_id=0, has_side_effects=True, vmem_limit_bytes=limit
        ),
        name="exchange",
    )(prior_cov, observed_index.reshape(1, NOBS), k, velocity, q, innov_factor)
    return pl.pallas_call(
        kd,
        out_shape=shape((ROWS, COLS), F32),
        in_specs=[VM],
        out_specs=ANY,
        scratch_shapes=[pltpu.SemaphoreType.DMA((LT,))],
        compiler_params=pltpu.CompilerParams(vmem_limit_bytes=8 * 1024 * 1024),
        name="place",
    )(p)


def solution(mesh):
    return jax.shard_map(
        on_device,
        mesh=mesh,
        in_specs=(P("row", "col"), P(), P(), P(), P(), P()),
        out_specs=P("row", "col"),
        check_vma=False,
    )
```

```python
import functools

import jax
import jax.numpy as jnp
from jax import lax
from jax.experimental import pallas as pl
from jax.experimental.pallas import tpu as pltpu
from jax.sharding import PartitionSpec as P

GX = 128
GY = 128
NOBS = 256
ROWS = 2048
COLS = 512
LT = 4
F32 = jnp.float32
BF = jnp.bfloat16
MESH = pl.DeviceIdType.MESH
PAD = 8
VM = pl.BlockSpec(memory_space=pltpu.VMEM)
ANY = pl.BlockSpec(memory_space=pl.ANY)


def split2(v):
    hi = v.astype(BF)
    return hi, (v - hi.astype(F32)).astype(BF)


def dot3(a, b, dims):
    (ah, al), (bh, bl) = split2(a), split2(b)
    dg = functools.partial(
        lax.dot_general, dimension_numbers=(dims, ((), ())), preferred_element_type=F32
    )
    return dg(ah, bh) + (dg(ah, bl) + dg(al, bh))


def fill_coefficients(k_ref, vel_ref, q_ref, speed, cf):
    for j in range(2):
        for g in range(GX):
            speed[j, g : g + 1, :] = vel_ref[j : j + 1, GY * g : GY * (g + 1)]
    k, a, b = k_ref[...], speed[0], speed[1]
    lane = lax.broadcasted_iota(jnp.int32, (GX, GY), 1)
    east = jnp.where(lane < GY - 1, k - 0.5 * a, 0.0)
    west = jnp.where(lane > 0, k + 0.5 * a, 0.0)
    parts = [
        1.0 - 4.0 * k,
        k + 0.5 * b,
        k - 0.5 * b,
        east,
        west,
        q_ref[...],
        pltpu.roll(east, 1, 1),
        pltpu.roll(west, GY - 1, 1),
    ]
    for j, part in enumerate(parts):
        cf[j, 0:PAD] = jnp.zeros((PAD, GY), F32)
        cf[j, PAD : PAD + GX] = part
        cf[j, PAD + GX :] = jnp.zeros((PAD, GY), F32)


def spread_rows(cf, tile, first, count, out_ref):
    def body(g, _):
        for j in range(5):
            tile[j : j + 1, :] = cf[j, pl.ds(first + g, 1), :]
        turned = jnp.transpose(tile[...])
        for j in range(5):
            out_ref[j, pl.ds(pl.multiple_of(g * GY, GY), GY), :] = jnp.broadcast_to(
                turned[:, j : j + 1], (GY, GY)
            )
        return 0

    lax.fori_loop(0, count, body, 0)


def row_step(src, coef, base, lt, lead):
    at = pl.multiple_of(base + lead, 8)
    mid = src[lt, pl.ds(at, 8), :]
    north = src[lt, pl.ds(pl.multiple_of(at - GY, 8), 8), :]
    south = src[lt, pl.ds(pl.multiple_of(at + GY, 8), 8), :]
    east = src[lt, pl.ds(at + 1, 8), :]
    west = src[lt, pl.ds(at - 1, 8), :]
    return (coef[0] * mid + coef[1] * north) + (coef[2] * south + (coef[3] * east + coef[4] * west))


def col_two_steps(tiles, coef_ref, first):
    def step(v, g):
        c = [coef_ref[j, pl.ds(first + g, 1), :] for j in range(5)]
        east = pltpu.roll(v[g], GY - 1, 1)
        west = pltpu.roll(v[g], 1, 1)
        return (c[0] * v[g] + c[1] * v[g - 1]) + (c[2] * v[g + 1] + (c[3] * east + c[4] * west))

    v1 = {g: step(tiles, g) for g in range(-1, 5)}
    return [step(v1, g) for g in range(4)]


def observe(obs_ref, cf, oc, w, ext, t_ref, r):
    for h in range(2):
        ids = jnp.broadcast_to(obs_ref[:, GY * h : GY * (h + 1)].astype(F32), (8, GY))
        oc[GY * h : GY * (h + 1), :] = jnp.broadcast_to(
            jnp.transpose(ids)[:, 0:1], (GY, GY)
        ).astype(jnp.int32)
    lane = lax.broadcasted_iota(jnp.int32, (32, GY), 1)
    first = PAD + 16 * r

    def step(before, v, after, g):
        at = lambda j, n: cf[j, pl.ds(first + n, 1), :]
        east = pltpu.roll(v, GY - 1, 1)
        west = pltpu.roll(v, 1, 1)
        return (at(0, g) * v + at(2, g - 1) * before) + (
            at(1, g + 1) * after + (at(7, g) * east + at(6, g) * west)
        )

    def body(i, _):
        rows = pl.ds(pl.multiple_of(i * 32, 32), 32)
        ids = oc[rows, :] - lane
        e = {g: jnp.where(ids == (16 * r + g) * GY, 1.0, 0.0) for g in range(-2, 18)}
        u = {g: step(e[g - 1], e[g], e[g + 1], g) for g in range(-1, 17)}
        for g in range(16):
            w[rows, GY * g : GY * (g + 1)] = step(u[g - 1], u[g], u[g + 1], g)
        return 0

    lax.fori_loop(0, NOBS // 32, body, 0)
    for n in range(4):
        rows = pl.ds(512 * n, 512)
        block = jnp.concatenate([ext[2 + lt, rows, :] for lt in range(LT)], axis=1)
        t = dot3(w[:, 512 * n : 512 * (n + 1)], block, ((1,), (0,)))
        for lt in range(LT):
            part = t[:, lt * GY : (lt + 1) * GY]
            t_ref[lt] = part if n == 0 else t_ref[lt] + part


PIECES = (0, 1792, 256, 512, 768, 1024, 1280, 1536)


def ka(
    c_ref,
    obs_ref,
    k_ref,
    vel_ref,
    q_ref,
    f_ref,
    p_ref,
    ext,
    v,
    v1,
    out,
    spread,
    cf,
    speed,
    tile,
    oc,
    w,
    t_ref,
    pc,
    pr,
    rs,
    psum,
    zin,
    text,
    relay1,
    relay2,
    hsend,
    hrecv,
    send,
    recv,
    local,
):
    r = lax.axis_index("row")
    c = lax.axis_index("col")
    zh, x = r // 4, r % 4
    y, zl, k = c // 8, (c % 8) // 2, c % 2
    no = jnp.logical_not
    x_edge = jnp.where(zh == 0, 3, 0)
    has_left, has_right = c > 0, c < 31
    c_left, c_right = jnp.maximum(c - 1, 0), jnp.minimum(c + 1, 31)
    left, right, partner = (r, c_left), (r, c_right), (4 * (1 - zh) + x, c)
    x_peers = [(4 * zh + (x + d) % 4, c) for d in (1, 2, 3)]
    y_peers = [(r, 8 * ((y + d) % 4) + 2 * zl + k) for d in (1, 2, 3)]
    z_peers = [(r, 8 * y + 2 * ((zl + d) % 4) + k) for d in (1, 2, 3)]
    core = (r, c + 1 - 2 * k)
    x_to = 2 * (y - 2 * zh) + zl // 2
    keeps = (y // 2 == zh) & (x_to == x) & (y == x)
    gives = (y // 2 == zh) & no(keeps)
    give_to = (4 * zh + jnp.where(gives, x_to, x), 8 * x + 2 * zl + k)
    y_from = 2 * zh + x // 2
    pair = x % 2
    holder = zl // 2 == pair
    near = zl == 2 - pair
    far = no(holder | near)
    takes = holder & no((y_from == y) & (x == y))
    take_from = (4 * zh + y, 8 * y_from + 2 * zl + k)
    s = zl % 2
    near_z = (r, 8 * y + 2 * (2 - pair) + k)
    far_z = (r, 8 * y + 6 * (1 - pair) + k)
    twin_z = (r, 8 * y + 2 * (zl + 1 - 2 * s) + k)

    def remote(src, dst, i, j, device, h=0):
        return pltpu.make_async_remote_copy(
            src_ref=src,
            dst_ref=dst,
            send_sem=send.at[h, i],
            recv_sem=recv.at[h, j],
            device_id=device,
            device_id_type=MESH,
        )

    halves = range(2)

    def rows_of(h, n):
        return pl.ds(pl.multiple_of(128 * h + 32 * n, 32), 32)

    barrier = pltpu.get_barrier_semaphore()

    def greet(*devices):
        for device in devices:
            pl.semaphore_signal(barrier, inc=1, device_id=device, device_id_type=MESH)

    greet(*x_peers, *y_peers, *z_peers, partner, core)
    pl.when(has_left)(lambda: greet(left))
    pl.when(has_right)(lambda: greet(right))
    pl.when(gives)(lambda: greet(give_to))
    pl.when(takes)(lambda: greet(take_from))
    one = lambda flag: jnp.where(flag, 1, 0)
    pl.semaphore_wait(
        barrier, 11 + one(has_left) + one(has_right) + one(gives) + one(takes)
    )

    def halo_out(side, piece, t):
        rows = pl.ds(PIECES[piece], 256)
        sem = side * 16 + piece * 2 + t
        return pltpu.make_async_remote_copy(
            src_ref=c_ref.at[rows, pl.ds(GY * t + (256 if side == 1 else 0), GY)],
            dst_ref=ext.at[t + (0 if side == 1 else 6), rows],
            send_sem=hsend.at[sem],
            recv_sem=hrecv.at[sem],
            device_id=right if side == 1 else left,
            device_id_type=MESH,
        )

    flags = {0: (has_left, has_right), 1: (has_right, has_left)}

    def halo_start(piece):
        for side in (0, 1):

            @pl.when(flags[side][0])
            def _():
                for t in (0, 1):
                    halo_out(side, piece, t).start()

    first = PAD + 4 * c

    def transport(piece):
        for side in (0, 1):

            @pl.when(flags[side][1])
            def _():
                for t in (0, 1):
                    halo_out(side, piece, t).wait_recv()

        def body(i, _):
            at = pl.ds(pl.multiple_of(PIECES[piece] + i * 16, 16), 16)
            to = pl.ds(pl.multiple_of(PIECES[piece] + 256 + i * 16, 16), 16)
            res = col_two_steps({g - 2: ext[g, at, :] for g in range(8)}, cf, first)
            for lt in range(LT):
                v[lt, to, :] = res[lt]
            return 0

        lax.fori_loop(0, 256 // 16, body, 0, unroll=2)

    def along_rows(one, two):
        def step_one(i, _):
            base = pl.multiple_of(i * 8, 8)
            coef = [spread[j, pl.ds(base, 8), :] for j in range(5)]
            for lt in range(LT):
                v1[lt, pl.ds(base, 8), :] = row_step(v, coef, base, lt, GY)
            return 0

        def step_two(i, _):
            base = pl.multiple_of(i * 8, 8)
            at = pl.ds(base, 8)
            coef = [spread[j, pl.ds(pl.multiple_of(base + GY, 8), 8), :] for j in range(5)]
            for lt in range(LT):
                out[lt, at, :] = out[lt, at, :] + row_step(v1, coef, base, lt, GY)
            return 0

        if one:
            lax.fori_loop((one[0] + 1) * 16, (one[1] + 1) * 16, step_one, 0, unroll=4)
        if two:
            lax.fori_loop(two[0] * 16, two[1] * 16, step_two, 0, unroll=4)

    def begin_out():
        def clear(i, _):
            for lt in range(LT):
                out[lt, pl.ds(pl.multiple_of(i * 64, 64), 64), :] = jnp.zeros((64, GY), F32)
            return 0

        lax.fori_loop(0, ROWS // 64, clear, 0)

        @pl.when(c // 4 == r)
        def _():
            i0 = lax.broadcasted_iota(jnp.int32, (GY, GY), 0)
            i1 = lax.broadcasted_iota(jnp.int32, (GY, GY), 1)
            for lt in range(LT):
                at = pl.ds(pl.multiple_of(512 * (c % 4) + GY * lt, GY), GY)
                noise = jnp.broadcast_to(cf[5, pl.ds(first + lt, 1), :], (GY, GY))
                out[lt, at, :] = jnp.where(i0 == i1, noise, 0.0)

    def subtract(kk, s_, weights):
        ci = 2 * s_ + kk
        lhs = jnp.concatenate([pr[kk, s_, lt] for lt in range(LT)], axis=1)
        u = dot3(lhs, weights, ((0,), (0,)))
        at = pl.ds(pl.multiple_of(512 * ci, 512), 512)
        for lt in range(LT):
            out[lt, at, :] = out[lt, at, :] - u[:, lt * GY : (lt + 1) * GY]

    halo_start(0)
    halo_start(1)
    inner = [
        pltpu.make_async_copy(c_ref.at[:, pl.ds(GY * t, GY)], ext.at[2 + t], local.at[t])
        for t in range(LT)
    ]
    for copy in inner:
        copy.start()
    halo_start(2)
    fill_coefficients(k_ref, vel_ref, q_ref, speed, cf)
    for copy in inner:
        copy.wait()
    observe(obs_ref, cf, oc, w, ext, t_ref, r)

    def rs_copy(h, d):
        there = rows_of(h, (x + d + 1) % 4)
        return remote(t_ref.at[:, there, :], rs.at[h, d], 12 + d, 12 + d, x_peers[d], h)

    for h in halves:
        for d in range(3):
            rs_copy(h, d).start()
    halo_start(3)
    for side, tiles in ((0, (6, 7)), (1, (0, 1))):

        @pl.when(no(flags[side][1]))
        def _():
            for t in tiles:
                ext[t] = jnp.zeros((ROWS, GY), F32)
                for h in halves:
                    text[h, t] = jnp.zeros((32, GY), F32)

    transport(0)
    transport(1)
    top, bottom = pl.ds(256, 256), pl.ds(2048, 256)
    above, below = pl.ds(0, 256), pl.ds(2304, 256)
    up_near, down_near = x > 0, x < 3
    up_to = (4 * zh + jnp.maximum(x - 1, 0), c)
    down_to = (4 * zh + jnp.minimum(x + 1, 3), c)
    up_copy = remote(v.at[:, top], v.at[:, below], 16, 16, up_to)
    down_copy = remote(v.at[:, bottom], v.at[:, above], 17, 17, down_to)
    pl.when(up_near)(lambda: up_copy.start())
    pl.when(down_near)(lambda: down_copy.start())
    at_edge = x == x_edge
    edge = (4 * zh + x_edge, c)
    cross = pl.ds(pl.multiple_of(jnp.where(zh == 0, 2048, 256), 256), 256)
    into = pl.ds(pl.multiple_of(jnp.where(zh == 0, 2304, 0), 256), 256)
    hop1 = [remote(v.at[j, cross], relay1, 18 + j, 18, (4 * zh + j, c)) for j in range(4)]
    keep1 = pltpu.make_async_copy(v.at[x, cross], relay1, local.at[4])

    @pl.when(at_edge)
    def _():
        for j, copy in enumerate(hop1):
            pl.when(x != j)(lambda copy=copy: copy.start())
        keep1.start()

    whole, low, high = pl.ds(2, 4), pl.ds(2, 2), pl.ds(4, 2)
    before, after = pl.ds(0, 2), pl.ds(6, 2)
    z_copy, to_right, to_left = [], [], []
    for h in halves:
        for d in range(3):
            rs_copy(h, d).wait()
        for lt in range(LT):
            text[h, 2 + lt] = (t_ref[lt, rows_of(h, x), :] + rs[h, 0, lt]) + (
                rs[h, 1, lt] + rs[h, 2, lt]
            )
        z_copy.append(remote(text.at[h, whole], zin.at[h], 15, 15, partner, h))
        to_right.append(remote(text.at[h, high], text.at[h, before], 22, 22, right, h))
        to_left.append(remote(text.at[h, low], text.at[h, after], 23, 23, left, h))
        z_copy[h].start()

    halo_start(4)
    spread_rows(cf, tile, PAD + 16 * r - 1, 18, spread)
    for h in halves:
        z_copy[h].wait()
        for lt in range(LT):
            text[h, 2 + lt] = text[h, 2 + lt] + zin[h, lt]
        pl.when(has_right)(lambda: to_right[h].start())
        pl.when(has_left)(lambda: to_left[h].start())
    begin_out()

    a_copy, a_keep, p_copy = [], [], []
    for h in halves:
        pl.when(has_left)(lambda: to_right[h].wait_recv())
        pl.when(has_right)(lambda: to_left[h].wait_recv())
        for i in range(2):
            at = pl.ds(16 * i, 16)
            total = {g - 2: text[h, g, at, :] for g in range(8)}
            res = col_two_steps(total, cf, first)
            my_obs = oc[pl.ds(pl.multiple_of(128 * h + 32 * x + 16 * i, 16), 16), :]
            for lt in range(LT):
                ids = c * COLS + lt * GY + lax.broadcasted_iota(jnp.int32, (16, GY), 1)
                noise = jnp.broadcast_to(cf[5, pl.ds(first + lt, 1), :], (16, GY))
                psum[h, lt, at, :] = res[lt] + jnp.where(my_obs == ids, noise, 0.0)
        a_copy.append(remote(psum.at[h], pr.at[k, s, :, rows_of(h, x)], 28, 28, give_to, h))
        a_keep.append(
            pltpu.make_async_copy(psum.at[h], pr.at[k, s, :, rows_of(h, x)], local.at[13 + h])
        )
        pl.when(gives)(lambda: a_copy[h].start())
        pl.when(keeps)(lambda: a_keep[h].start())
    for h in halves:
        for d in range(3):
            p_copy.append(
                remote(psum.at[h], pc.at[:, rows_of(h, x)], 25 + d, 25 + d, x_peers[d], h)
            )
            p_copy[-1].start()
        for lt in range(LT):
            pc[lt, rows_of(h, x), :] = psum[h, lt]

    hop2 = remote(relay1, relay2, 24, 24, partner)
    pl.when(at_edge)(lambda: keep1.wait())
    pl.when(no(at_edge))(lambda: hop1[0].wait_recv())
    hop2.start()
    transport(2)

    t0 = jnp.where(holder, s, 1 - pair)
    kinds = (t0, 1 - t0)

    def part(h, i, d, kk):
        return pr.at[kk, kinds[i], :, rows_of(h, (y + 4 - d) % 4)]

    piece = [pr.at[k, s, :, rows_of(h, y)] for h in halves]
    a_wait = [remote(psum.at[h], piece[h], 28, 28, give_to, h) for h in halves]
    b_twin = [remote(piece[h], piece[h], 29, 30, twin_z, h) for h in halves]
    second = jnp.where(s == 1 - pair, 0, 1)
    b_near = [remote(piece[h], piece[h], 30, 29 + second, near_z, h) for h in halves]
    arrive = [
        [remote(part(h, i, 0, k), part(h, i, 0, k), 31 + i, 29 + i, far_z, h) for i in range(2)]
        for h in halves
    ]

    def along_y(h, i, d):
        n = 33 + 2 * d + i
        return remote(part(h, i, 0, k), part(h, i, 0, k), n, n, y_peers[d], h)

    def y_in(h, i, d):
        n = 33 + 2 * d + i
        return remote(part(h, i, d + 1, k), part(h, i, d + 1, k), n, n, y_peers[d], h)

    def to_core(h, i, d):
        n = 40 + 2 * d + i
        return remote(part(h, i, d, k), part(h, i, d, k), n, n, core, h)

    def core_in(h, i, d):
        n = 40 + 2 * d + i
        return remote(part(h, i, d, 1 - k), part(h, i, d, 1 - k), n, n, core, h)

    def pass_on(h, i):
        pl.when(near)(lambda: arrive[h][i].start())
        for d in range(3):
            along_y(h, i, d).start()
        to_core(h, i, 0).start()

    for h in halves:

        @pl.when(holder)
        def _():
            pl.when(takes)(lambda: a_wait[h].wait_recv())
            pl.when(no(takes))(lambda: a_keep[h].wait())
            b_near[h].start()
            b_twin[h].start()

        @pl.when(no(holder))
        def _():
            arrive[h][0].wait_recv()

        pass_on(h, 0)
    halo_start(5)
    for h in halves:
        arrive[h][1].wait_recv()
        pass_on(h, 1)

    halo_start(6)
    halo_start(7)

    transport(3)
    along_rows((1, 5), (2, 4))
    hop2.wait_recv()
    last = pltpu.make_async_copy(relay2, v.at[x, into], local.at[6])
    pl.when(at_edge)(lambda: last.start())

    def forward(j):
        return remote(relay2, v.at[j, into], 39, 52 + j, edge)

    for j in range(4):
        pl.when(no(at_edge) & (x == j))(lambda j=j: forward(j).start())

    for i in range(2):
        for h in halves:
            for d in range(3):
                y_in(h, i, d).wait_recv()
                to_core(h, i, d + 1).start()
        transport(4 + i)
        along_rows((5 + 2 * i, 7 + 2 * i), (4 + 2 * i, 6 + 2 * i))
    for copy in p_copy:
        copy.wait_recv()
    f = f_ref[...]
    gain = dot3(f, f, ((0,), (0,)))
    weights = dot3(gain, jnp.concatenate([pc[lt] for lt in range(LT)], axis=1), ((1,), (0,)))
    for i in range(2):
        subtract(k, i, weights)
    transport(6)
    along_rows((9, 11), (8, 10))
    for h in halves:
        for i in range(2):
            for d in range(4):
                core_in(h, i, d).wait_recv()
    for i in range(2):
        subtract(1 - k, i, weights)

    def store(n):
        rows = pl.ds(*((256, 1024), (1280, 768), (0, 256))[n])
        return pltpu.make_async_copy(out.at[:, rows], p_ref.at[:, rows], local.at[7 + n])

    store(0).start()
    transport(7)
    along_rows((11, 15), (10, 14))
    pl.when(down_near)(lambda: up_copy.wait_recv())
    pl.when(up_near)(lambda: down_copy.wait_recv())

    @pl.when(at_edge)
    def _():
        last.wait()
        for j in range(4):
            pl.when(x != j)(lambda j=j: forward(j).wait_recv())

    for flag, rows in ((r == 0, above), (r == 7, below)):

        @pl.when(flag)
        def _():
            for lt in range(LT):
                v[lt, rows, :] = jnp.zeros((256, GY), F32)

    along_rows((15, 17), (14, 16))
    store(1).start()
    along_rows((-1, 1), (0, 2))
    store(2).start()

    for n in range(3):
        store(n).wait()
    pl.when(up_near)(lambda: up_copy.wait_send())
    pl.when(down_near)(lambda: down_copy.wait_send())

    @pl.when(at_edge)
    def _():
        for j, copy in enumerate(hop1):
            pl.when(x != j)(lambda copy=copy: copy.wait_send())

    hop2.wait_send()
    pl.when(no(at_edge))(lambda: forward(0).wait_send())

    @pl.when(has_right)
    def _():
        for copy in to_right:
            copy.wait_send()

    @pl.when(has_left)
    def _():
        for copy in to_left:
            copy.wait_send()

    for copy in p_copy:
        copy.wait_send()
    for h in halves:
        pl.when(gives)(lambda: a_copy[h].wait_send())
        pl.when(keeps & no(holder))(lambda: a_keep[h].wait())

        @pl.when(holder)
        def _():
            b_near[h].wait_send()
            b_twin[h].wait_send()

        for i in range(2):
            pl.when(near)(lambda: arrive[h][i].wait_send())
            for d in range(3):
                along_y(h, i, d).wait_send()
            for d in range(4):
                to_core(h, i, d).wait_send()
    for side in (0, 1):

        @pl.when(flags[side][0])
        def _():
            for n in range(len(PIECES)):
                for t in (0, 1):
                    halo_out(side, n, t).wait_send()


def kd(p_in, o_ref, p, sem, osem):
    chunks = [(lt, pl.ds(1024 * n, 1024)) for n in range(2) for lt in range(LT)]
    loads = [
        pltpu.make_async_copy(p_in.at[lt, at], p.at[lt, at], sem.at[n])
        for n, (lt, at) in enumerate(chunks)
    ]
    stores = [
        pltpu.make_async_copy(p.at[lt, at], o_ref.at[at, pl.ds(GY * lt, GY)], osem.at[n])
        for n, (lt, at) in enumerate(chunks)
    ]
    for copy in loads:
        copy.start()
    for load, put in zip(loads, stores):
        load.wait()
        put.start()
    for copy in stores:
        copy.wait()


def on_device(prior_cov, diffusivity, velocity, variance, observed_index, innov_factor):
    shape = jax.ShapeDtypeStruct
    limit = 60 * 1024 * 1024
    k = diffusivity.reshape(GX, GY)
    q = variance.reshape(GX, GY)
    p = pl.pallas_call(
        ka,
        out_shape=shape((LT, ROWS, GY), F32),
        in_specs=[ANY] + [VM] * 5,
        out_specs=ANY,
        scratch_shapes=[
            pltpu.VMEM((8, ROWS, GY), F32),
            pltpu.VMEM((LT, 2560, GY), F32),
            pltpu.VMEM((LT, 2304, GY), F32),
            pltpu.VMEM((LT, ROWS, GY), F32),
            pltpu.VMEM((5, 2304, GY), F32),
            pltpu.VMEM((8, GX + 2 * PAD, GY), F32),
            pltpu.VMEM((2, GX, GY), F32),
            pltpu.VMEM((8, GY), F32),
            pltpu.VMEM((NOBS, GY), jnp.int32),
            pltpu.VMEM((NOBS, ROWS), F32),
            pltpu.VMEM((LT, NOBS, GY), F32),
            pltpu.VMEM((LT, NOBS, GY), F32),
            pltpu.VMEM((2, 2, LT, NOBS, GY), F32),
            pltpu.VMEM((2, 3, LT, 32, GY), F32),
            pltpu.VMEM((2, LT, 32, GY), F32),
            pltpu.VMEM((2, LT, 32, GY), F32),
            pltpu.VMEM((2, 8, 32, GY), F32),
            pltpu.VMEM((256, GY), F32),
            pltpu.VMEM((256, GY), F32),
            pltpu.SemaphoreType.DMA((32,)),
            pltpu.SemaphoreType.DMA((32,)),
            pltpu.SemaphoreType.DMA((2, 56)),
            pltpu.SemaphoreType.DMA((2, 56)),
            pltpu.SemaphoreType.DMA((15,)),
        ],
        compiler_params=pltpu.CompilerParams(
            collective_id=0, has_side_effects=True, vmem_limit_bytes=limit
        ),
        name="exchange",
    )(prior_cov, observed_index.reshape(1, NOBS), k, velocity, q, innov_factor)
    return pl.pallas_call(
        kd,
        out_shape=shape((ROWS, COLS), F32),
        in_specs=[ANY],
        out_specs=ANY,
        scratch_shapes=[
            pltpu.VMEM((LT, ROWS, GY), F32),
            pltpu.SemaphoreType.DMA((8,)),
            pltpu.SemaphoreType.DMA((8,)),
        ],
        compiler_params=pltpu.CompilerParams(vmem_limit_bytes=limit),
        name="place",
    )(p)


def solution(mesh):
    return jax.shard_map(
        on_device,
        mesh=mesh,
        in_specs=(P("row", "col"), P(), P(), P(), P(), P()),
        out_specs=P("row", "col"),
        check_vma=False,
    )
```
